128 devices in a mesh: row: 8 (over y, x_hi), col: 16 (over x_lo, z, core).
Axes of the slice: x: 4 (x_hi: 2, x_lo: 2; x = x_hi * 2 + x_lo), y: 4, z: 4, core: 2. Of those that a mesh axis runs over, the one named last changes fastest.
Arguments:
- local_ops: bfloat16 [8, 16, 2048, 2048], P('row', 'col'), may hold values from -2 to 30, as said below
- loads: float32 [8, 16, 2048, 256], P('row', 'col'), may hold values from -6 to 6
- modes: float32 [8, 16, 32, 2048], P('row', 'col'), may hold values from -1 to 1
- coarse_inverse: float32 [4096, 4096], P('row', 'col'), may hold values from -1 to 1
- face_rows: int32 [8, 16, 4, 512], P('row', 'col'), may hold values from 0 to 2047, as said below
- adjacency: int32 [8, 16, 4], P('row', 'col'), may hold values from 0 to 1, as said below
- contact: int32 [8, 16, 2048], P('row', 'col'), may hold values 0 or 1
Outputs:
- multipliers: float32 [8, 16, 2048, 256], P('row', 'col')
The draws below stay inside these ranges and needn't reach their ends.
Inputs may be any that keep to these rules, and one draw needn't show every extreme that they name: `face_rows`: for each subdomain the 2048 entries are a permutation of 0 to 2047. `adjacency`: symmetric across each shared face (a subdomain's south flag equals the north flag of the one below it, its east flag the west flag of the one to its right); 0 on faces at the grid's edge. `local_ops`: each subdomain's local dual operator is symmetric positive definite.
All inputs are finite; a program needn't handle non-finite values. No bound on the sum of `contact` on one device may be relied on, other than what follows from the above.
Results may differ from the reference program's by a relative error of at most 0.00099.
Values sent between devices are 32-bit elements; how exact they have to be, the bound alone decides.
A program may use at most 128 MiB of HBM per device.

```python
import jax
import jax.numpy as jnp
from jax import lax

M = 2048
NM = 32
K = 256
ITERS = 2
FACE = 512
GRID_ROWS = 8
GRID_COLS = 16
NCO = 4096


def draw_local_ops(key, part):
    subdomains = GRID_ROWS * GRID_COLS
    base_key = jax.random.fold_in(key, 101)

    def draw_one(position):
        sub_key = jax.random.fold_in(base_key, position)
        first_key, second_key = jax.random.split(sub_key)
        ratio = position.astype(jnp.float32) / max(subdomains - 1, 1)
        factor = 3.0 ** ratio
        noise_part = jnp.clip(jax.random.normal(first_key, (M, M), jnp.float32), -4.0, 4.0)
        symmetric = (noise_part + noise_part.T) * 0.70710678
        diagonal = jnp.exp(jax.random.uniform(second_key, (M,), jnp.float32, jnp.log(1.2), jnp.log(3.0)))
        matrix = factor * (0.45 / M ** 0.5 * symmetric + jnp.diag(diagonal))
        return matrix.astype(jnp.bfloat16)
    stacked = lax.map(draw_one, jnp.arange(subdomains, dtype=jnp.int32))
    return stacked.reshape(GRID_ROWS, GRID_COLS, M, M)


def draw_coarse_inverse(key, part):
    sub_key = jax.random.fold_in(key, 202)
    noise_part = jnp.clip(jax.random.normal(sub_key, (NCO, NCO), jnp.float32), -4.0, 4.0)
    scale_value = 0.5 * (NM / M) ** 0.5
    return scale_value * (jnp.eye(NCO, dtype=jnp.float32) + 0.6 * noise_part / NCO ** 0.5)


def draw_face_rows(key, part):
    key_list = jax.random.split(jax.random.fold_in(key, 303), GRID_ROWS * GRID_COLS)

    def permute_one(sub_key):
        return jax.random.permutation(sub_key, M).astype(jnp.int32)
    permuted = jax.vmap(permute_one)(key_list)
    return permuted.reshape(GRID_ROWS, GRID_COLS, 4, FACE).astype(jnp.int32)


def draw_adjacency(key, part):
    first_key, second_key = jax.random.split(jax.random.fold_in(key, 404))
    vertical = (jax.random.randint(first_key, (GRID_ROWS, GRID_COLS), 0, 4) < 3).astype(jnp.int32)
    lateral = (jax.random.randint(second_key, (GRID_ROWS, GRID_COLS), 0, 4) < 3).astype(jnp.int32)
    vertical = vertical.at[GRID_ROWS - 1, :].set(0)
    lateral = lateral.at[:, GRID_COLS - 1].set(0)
    north = jnp.concatenate([jnp.zeros((1, GRID_COLS), jnp.int32), vertical[:-1]], axis=0)
    west = jnp.concatenate([jnp.zeros((GRID_ROWS, 1), jnp.int32), lateral[:, :-1]], axis=1)
    return jnp.stack([north, vertical, west, lateral], axis=-1).astype(jnp.int32)


def set_ends(drawn, rng, least, high):
    place = [jax.random.randint(jax.random.fold_in(rng, axis), (), 0, length) for axis, length in enumerate(drawn.shape)]
    main_axis = drawn.shape.index(max(drawn.shape))
    neighbour = place[:main_axis] + [(place[main_axis] + 1) % drawn.shape[main_axis]] + place[main_axis + 1:]
    return drawn.at[tuple(place)].set(least).at[tuple(neighbour)].set(high)


def steps_of(own_key, extent, cuts, low, largest):
    def one(dim, shards_of):
        heights = jax.random.uniform(jax.random.fold_in(jax.random.fold_in(own_key, 6), dim), (shards_of,), jnp.float32, low / len(cuts), largest / len(cuts))
        return jnp.repeat(jnp.exp(heights), extent[dim] // shards_of).reshape((-1,) + (1,) * (len(extent) - dim - 1))

    loudness = one(*cuts[0])
    for cut in cuts[1:]:
        loudness = loudness * one(*cut)
    return loudness


def normal_values(rng, extent, spread, bound, cuts=(), held_as=jnp.bfloat16):
    loudness = steps_of(rng, extent, cuts, -0.22, 0.18) if cuts else 1.0
    drawn = jax.random.normal(rng, extent, jnp.float32) * spread * loudness
    return jnp.minimum(jnp.maximum(drawn, -bound), bound).astype(held_as)


def setup_inputs(seed: int = 0) -> dict:
    keys = jax.random.split(jax.random.key(seed), 8)
    return {
        "local_ops": draw_local_ops(jax.random.fold_in(keys[7], 71), 0),
        "loads": normal_values(keys[1], (GRID_ROWS, GRID_COLS, M, K), 1.0, 6.0, ((0, 8), (1, 16)), jnp.float32),
        "modes": normal_values(keys[2], (GRID_ROWS, GRID_COLS, NM, M), NM ** -0.5, 1.0, ((0, 8), (1, 16)), jnp.float32),
        "coarse_inverse": draw_coarse_inverse(jax.random.fold_in(keys[7], 71), 0),
        "face_rows": draw_face_rows(jax.random.fold_in(keys[7], 71), 0),
        "adjacency": draw_adjacency(jax.random.fold_in(keys[7], 71), 0),
        "contact": set_ends((jax.random.randint(keys[6], (GRID_ROWS, GRID_COLS, M), 0, 2) < 1).astype(jnp.int32), jax.random.fold_in(keys[6], 1), 0, 1),
    }


def face_blocks(field_values, face_rows):
    def pick_rows(values, indices):
        return values[indices]
    return jax.vmap(jax.vmap(pick_rows))(field_values, face_rows)


def assemble(field_values, face_rows, adj_flags):
    blocks = face_blocks(field_values, face_rows)
    zero_row = jnp.zeros_like(blocks[:1, :, 0])
    north = jnp.concatenate([zero_row, blocks[:-1, :, 1]], axis=0)
    south = jnp.concatenate([blocks[1:, :, 0], zero_row], axis=0)
    zero_col = jnp.zeros_like(blocks[:, :1, 2])
    west = jnp.concatenate([zero_col, blocks[:, :-1, 3]], axis=1)
    east = jnp.concatenate([blocks[:, 1:, 2], zero_col], axis=1)
    incoming = jnp.stack([north, south, west, east], axis=2) * adj_flags[:, :, :, None, None]

    def add_rows(values, indices, incoming_rows):
        return values.at[indices.reshape(-1)].add(incoming_rows.reshape(-1, incoming_rows.shape[-1]))
    return jax.vmap(jax.vmap(add_rows))(field_values, face_rows, incoming)


def apply_ops(local_ops, field_values):
    grid_rows, grid_cols, order, _ = local_ops.shape
    flat_ops = local_ops.reshape(grid_rows * grid_cols, order, order)
    flat_vec = field_values.astype(jnp.bfloat16).reshape(grid_rows * grid_cols, order, -1)

    def product(operands):
        return jnp.dot(operands[0], operands[1], preferred_element_type=jnp.float32)
    return lax.map(product, (flat_ops, flat_vec)).reshape(field_values.shape)


def reference(local_ops, loads, modes, coarse_inverse, face_rows, adjacency, contact):
    adj_flags = adjacency.astype(jnp.float32)
    face_size = face_rows.shape[-1]
    free_face = jnp.repeat(1.0 - adj_flags, face_size, axis=-1)

    def place_values(indices, values):
        return jnp.zeros((loads.shape[2],), jnp.float32).at[indices.reshape(-1)].set(values)
    row_free = jax.vmap(jax.vmap(place_values))(face_rows, free_face)
    weight = 0.5 + 0.5 * row_free
    clamp_rows = contact.astype(jnp.float32) * row_free > 0.5
    multipliers = jnp.zeros(loads.shape, jnp.float32)
    for iteration in range(ITERS):
        if iteration == 0:
            local_term = -loads
        else:
            local_term = apply_ops(local_ops, multipliers) - loads
        gradient = assemble(local_term, face_rows, adj_flags)
        coarse_coef = jnp.einsum("abmr,abrk->abmk", modes, gradient, precision=lax.Precision.HIGHEST)
        case_count = coarse_coef.shape[-1]
        coarse_amount = jnp.dot(coarse_inverse, coarse_coef.reshape(-1, case_count), precision=lax.Precision.HIGHEST, preferred_element_type=jnp.float32).reshape(coarse_coef.shape)
        correction = jnp.einsum("abmr,abmk->abrk", modes, coarse_amount, precision=lax.Precision.HIGHEST)
        direction = gradient - assemble(correction, face_rows, adj_flags)
        operated = apply_ops(local_ops, direction)
        numerator = jnp.sum(weight[..., None] * direction * direction, axis=(0, 1, 2))
        denominator = jnp.sum(direction * operated, axis=(0, 1, 2))
        step_length = numerator / denominator
        multipliers = multipliers - step_length * direction
        multipliers = jnp.where(clamp_rows[..., None], jnp.maximum(multipliers, 0.0), multipliers)
    return multipliers
```

```python
import functools

import jax
import jax.numpy as jnp
from jax import lax
from jax.experimental import pallas as pl
from jax.experimental.pallas import tpu as pltpu
from jax.sharding import PartitionSpec as P

ITERS = 2
F32 = jnp.float32
BF16 = jnp.bfloat16
MESH = pl.DeviceIdType.MESH
LANES = 128
VMEM_BYTES = 63_000_000


def halves(value):
    high = value.astype(BF16)
    low = (value - high.astype(F32)).astype(BF16)
    return high, low


def mul(a, b):
    return jnp.dot(a, b, preferred_element_type=F32)


def mul_split(a, b):
    a_high, a_low = a
    b_high, b_low = b
    return mul(a_high, b_high) + (mul(a_high, b_low) + mul(a_low, b_high))


def wide(value):
    return jnp.concatenate([value, value], axis=1)


def by_eight(value):
    return value.reshape(value.shape[0] // 8, 8, value.shape[1]).sum(axis=0)


def kernel(
    rows,
    cols,
    adj_ref,
    modes_ref,
    loads_ref,
    tile_ref,
    index_ref,
    contact_ref,
    op_hbm,
    out_ref,
    op_ref,
    pick,
    place,
    pieces,
    modes_high,
    modes_low,
    modes_high_t,
    modes_low_t,
    row_weight,
    row_clamp,
    field,
    direction,
    direction_half,
    mode_send,
    mode_recv,
    face_send,
    face_recv,
    product_send,
    product_recv,
    coef_send,
    coef_recv,
    part_send,
    part_recv,
    amount_send,
    amount_recv,
    first_send,
    first_recv,
    second_send,
    second_recv,
    op_sem,
    mode_sems,
    face_sems,
    product_sems,
    coef_sems,
    part_sems,
    amount_sems,
    first_sems,
    second_sems,
):
    row = lax.axis_index("row")
    col = lax.axis_index("col")
    order, cases = loads_ref.shape
    mode_count = modes_ref.shape[0]
    face = index_ref.shape[1]
    group = coef_recv.shape[1]
    step = 512
    blocks = order // step

    op_copy = pltpu.make_async_copy(op_hbm, op_ref, op_sem)
    op_copy.start()

    sides = (
        (row > 0, (row - 1, col)),
        (row < rows - 1, (row + 1, col)),
        (col > 0, (row, col - 1)),
        (col < cols - 1, (row, col + 1)),
    )
    coef_col = (row * cols + col) // group
    coef_slot = lax.rem(col, group)
    source_row = (col * group) // cols
    source_col = lax.rem(col * group, cols)
    at_home = coef_col == col

    barrier = pltpu.get_barrier_semaphore()
    for k in range(1, cols):
        pl.semaphore_signal(
            barrier, inc=1, device_id=(row, lax.rem(col + k, cols)), device_id_type=MESH
        )
    for k in range(1, rows):
        pl.semaphore_signal(
            barrier, inc=1, device_id=(lax.rem(row + k, rows), col), device_id_type=MESH
        )
    for k in range(group):
        is_me = (source_row == row) & (source_col + k == col)

        @pl.when(jnp.logical_not(is_me))
        def _():
            pl.semaphore_signal(
                barrier, inc=1, device_id=(source_row, source_col + k), device_id_type=MESH
            )

    for f in range(4):

        @pl.when(jnp.logical_not(sides[f][0]))
        def _():
            mode_recv[f] = jnp.zeros(mode_recv.shape[1:], F32)
            for it in range(ITERS):
                face_recv[it, f] = jnp.zeros(face_recv.shape[2:], F32)
                product_recv[it, f] = jnp.zeros(product_recv.shape[2:], F32)
                amount_recv[it, f] = jnp.zeros(amount_recv.shape[2:], F32)

    def side_copy(f, source, target, sems):
        return pltpu.make_async_remote_copy(
            src_ref=source,
            dst_ref=target.at[f ^ 1],
            send_sem=sems.at[0, f],
            recv_sem=sems.at[1, f ^ 1],
            device_id=sides[f][1],
            device_id_type=MESH,
        )

    def start_side(f, source, target, sems):
        @pl.when(sides[f][0])
        def _():
            side_copy(f, source, target, sems).start()

    def wait_side(f, target, sems):
        @pl.when(sides[f][0])
        def _():
            pltpu.make_async_remote_copy(
                src_ref=target.at[f],
                dst_ref=target.at[f],
                send_sem=sems.at[0, f],
                recv_sem=sems.at[1, f],
                device_id=sides[f][1],
                device_id_type=MESH,
            ).wait_recv()

    def sent_side(f, source, target, sems):
        @pl.when(sides[f][0])
        def _():
            side_copy(f, source, target, sems).wait_send()

    @pl.loop(0, order // 256)
    def _(i):
        at = pl.ds(pl.multiple_of(i * 256, 256), 256)
        for f in range(4):
            here = lax.broadcasted_iota(jnp.int32, (256, face), 0) + i * 256
            hit = here == index_ref[f : f + 1, :]
            place[at, f * face : (f + 1) * face] = jnp.where(hit, 1.0, 0.0).astype(BF16)

    high, low = halves(modes_ref[...])
    modes_high[0:mode_count] = high
    modes_low[0:mode_count] = low
    both = jnp.concatenate([high, low], axis=0)
    for f in range(4):
        moved = mul(both, place[:, f * face : (f + 1) * face])
        mode_send[f] = moved[0:mode_count] + moved[mode_count:]

    here = (source_row == row) & (source_col <= col) & (col < source_col + group)
    pl.semaphore_wait(barrier, cols - 1 + rows - 1 + group - here.astype(jnp.int32))
    for f in range(4):
        start_side(f, mode_send.at[f], mode_recv, mode_sems)

    for f in range(4):
        down = jnp.broadcast_to(index_ref[f : f + 1, :], (LANES, face)).T

        @pl.loop(0, order // LANES)
        def _(i):
            there = lax.broadcasted_iota(jnp.int32, (face, LANES), 1) + i * LANES
            at = pl.ds(pl.multiple_of(i * LANES, LANES), LANES)
            pick[f * face : (f + 1) * face, at] = jnp.where(down == there, 1.0, 0.0).astype(BF16)

    def each_block(body):
        @pl.loop(0, blocks)
        def _(i):
            body(pl.ds(pl.multiple_of(i * step, step), step))

    def negate(at):
        value = -loads_ref[at, :]
        field[at, :] = value
        high, low = halves(value)
        pieces[at, 0:cases] = high
        pieces[at, cases:] = low

    def faces_of_field(it):
        for f in range(4):
            moved = mul(pick[f * face : (f + 1) * face, :], pieces[...])
            face_send[it, f] = moved[:, 0:cases] + moved[:, cases:]

    def flag(f):
        return adj_ref[0, f].astype(F32)

    def fill_modes():
        for f in range(4):
            high, low = halves(mode_recv[f])
            moved = mul(
                jnp.concatenate([high, low], axis=0), pick[f * face : (f + 1) * face, :]
            )
            high, low = halves(moved[0:mode_count] + moved[mode_count:])
            at = slice((f + 1) * mode_count, (f + 2) * mode_count)
            modes_high[at] = high
            modes_low[at] = low
        modes_high_t[...] = modes_high[...].astype(F32).T.astype(BF16)
        modes_low_t[...] = modes_low[...].astype(F32).T.astype(BF16)

    def fill_rows():
        flags = jnp.concatenate(
            [jnp.full((face, LANES), flag(f), F32) for f in range(4)], axis=0
        ).astype(BF16)
        for i in range(blocks):
            glued = mul(place[i * step : (i + 1) * step, :], flags)
            touching = (
                jnp.broadcast_to(contact_ref[:, i * step : (i + 1) * step], (LANES, step))
                .astype(F32)
                .T
            )
            free = 1.0 - glued
            row_weight[i * step : (i + 1) * step, :] = 0.5 + 0.5 * free
            row_clamp[i * step : (i + 1) * step, :] = touching * free

    def clamped(at, value):
        return jnp.where(wide(row_clamp[at, :]) > 0.5, jnp.maximum(value, 0.0), value)

    def all_sum(it, totals):
        parts = cases // LANES
        tile = jnp.concatenate(
            [totals[t : t + 1, p * LANES : (p + 1) * LANES] for t in range(2) for p in range(parts)]
            + [jnp.zeros((8 - 2 * parts, LANES), F32)],
            axis=0,
        )
        first_send[it] = tile

        def first(k):
            return pltpu.make_async_remote_copy(
                src_ref=first_send.at[it],
                dst_ref=first_recv.at[it, k],
                send_sem=first_sems.at[it, 0, k],
                recv_sem=first_sems.at[it, 1, k],
                device_id=(row, lax.rem(col + k, cols)),
                device_id_type=MESH,
            )

        for k in range(1, cols):
            first(k).start()
        for k in range(1, cols):
            first(k).wait_recv()
        tile = tile + first_recv[it, 1:cols].sum(axis=0)
        second_send[it] = tile

        def second(k):
            return pltpu.make_async_remote_copy(
                src_ref=second_send.at[it],
                dst_ref=second_recv.at[it, k],
                send_sem=second_sems.at[it, 0, k],
                recv_sem=second_sems.at[it, 1, k],
                device_id=(lax.rem(row + k, rows), col),
                device_id_type=MESH,
            )

        for k in range(1, rows):
            second(k).start()
        for k in range(1, rows):
            second(k).wait_recv()
        tile = tile + second_recv[it, 1:rows].sum(axis=0)
        for k in range(1, cols):
            first(k).wait_send()
        for k in range(1, rows):
            second(k).wait_send()
        top = jnp.concatenate([tile[p : p + 1] for p in range(parts)], axis=1)
        low = jnp.concatenate([tile[parts + p : parts + p + 1] for p in range(parts)], axis=1)
        return top / low

    for it in range(ITERS):
        if it == 0:
            each_block(negate)
            faces_of_field(it)
            for f in range(4):
                wait_side(f, mode_recv, mode_sems)
            for f in range(4):
                mode_recv[f] = mode_recv[f] * flag(f)
            for f in range(4):
                product_send[it, f] = mul_split(halves(mode_recv[f]), halves(face_send[it, f]))
            for f in range(4):
                start_side(f, product_send.at[it, f], product_recv.at[it], product_sems.at[it])
            own = mul_split(
                (modes_high[0:mode_count], modes_low[0:mode_count]),
                (pieces[:, 0:cases], pieces[:, cases:]),
            )
        else:
            products = mul_split(
                (modes_high[...], modes_low[...]), (pieces[:, 0:cases], pieces[:, cases:])
            )
            own = products[0:mode_count]
            for f in range(4):
                product_send[it, f] = products[(f + 1) * mode_count : (f + 2) * mode_count]
            for f in range(4):
                start_side(f, product_send.at[it, f], product_recv.at[it], product_sems.at[it])
            faces_of_field(it)
        for f in range(4):
            wait_side(f, product_recv.at[it], product_sems.at[it])
            own = own + product_recv[it, f]
        coef_send[it] = own

        def coef(k):
            return pltpu.make_async_remote_copy(
                src_ref=coef_send.at[it],
                dst_ref=coef_recv.at[it, coef_slot],
                send_sem=coef_sems.at[it, 0, k],
                recv_sem=coef_sems.at[it, 1, coef_slot],
                device_id=(lax.rem(row + k, rows), coef_col),
                device_id_type=MESH,
            )

        for k in range(rows):
            if k == 0:

                @pl.when(at_home)
                def _():
                    coef_recv[it, coef_slot] = own

                @pl.when(jnp.logical_not(at_home))
                def _():
                    coef(0).start()

            else:
                coef(k).start()
        for f in range(4):
            start_side(f, face_send.at[it, f], face_recv.at[it], face_sems.at[it])
        if it == 0:
            fill_modes()
            fill_rows()
        for k in range(group):
            is_me = (source_row == row) & (source_col + k == col)

            @pl.when(jnp.logical_not(is_me))
            def _():
                pltpu.make_async_remote_copy(
                    src_ref=coef_send.at[it],
                    dst_ref=coef_recv.at[it, k],
                    send_sem=coef_sems.at[it, 0, 0],
                    recv_sem=coef_sems.at[it, 1, k],
                    device_id=(source_row, source_col + k),
                    device_id_type=MESH,
                ).wait_recv()

        block = coef_recv[it].reshape(group * mode_count, cases)
        part_send[it] = mul_split(halves(tile_ref[...]), halves(block)).reshape(
            cols, mode_count, cases
        )

        def part(k):
            target = lax.rem(col + k, cols)
            return pltpu.make_async_remote_copy(
                src_ref=part_send.at[it, target],
                dst_ref=part_recv.at[it, k],
                send_sem=part_sems.at[it, 0, k],
                recv_sem=part_sems.at[it, 1, k],
                device_id=(row, target),
                device_id_type=MESH,
            )

        for k in range(1, cols):
            part(k).start()
        for k in range(1, cols):
            part(k).wait_recv()
        amount = part_send[it, col] + part_recv[it, 1:cols].sum(axis=0)
        amount_send[it] = amount
        for f in range(4):
            start_side(f, amount_send.at[it], amount_recv.at[it], amount_sems.at[it])

        for f in range(4):
            wait_side(f, face_recv.at[it], face_sems.at[it])
            high, low = halves(face_recv[it, f] * flag(f))
            pieces[f * face : (f + 1) * face, 0:cases] = high
            pieces[f * face : (f + 1) * face, cases:] = low

        def add_faces(at):
            moved = mul(place[at, :], pieces[...])
            field[at, :] = field[at, :] + (moved[:, 0:cases] + moved[:, cases:])

        each_block(add_faces)
        for f in range(4):
            wait_side(f, amount_recv.at[it], amount_sems.at[it])
        amounts = halves(
            jnp.concatenate([amount] + [amount_recv[it, f] for f in range(4)], axis=0)
        )

        def turn(i, total):
            at = pl.ds(pl.multiple_of(i * step, step), step)
            value = field[at, :] - mul_split((modes_high_t[at, :], modes_low_t[at, :]), amounts)
            direction[at, :] = value
            direction_half[at, :] = value.astype(BF16)
            return total + by_eight(wide(row_weight[at, :]) * value * value)

        top = lax.fori_loop(0, blocks, turn, jnp.zeros((8, cases), F32))
        if it == 0:
            op_copy.wait()

        def operate(i, total):
            at = pl.ds(pl.multiple_of(i * step, step), step)
            return total + by_eight(direction[at, :] * mul(op_ref[at, :], direction_half[...]))

        low = lax.fori_loop(0, blocks, operate, jnp.zeros((8, cases), F32))
        totals = jnp.concatenate(
            [top.sum(axis=0, keepdims=True), low.sum(axis=0, keepdims=True)], axis=0
        )
        length = all_sum(it, totals)

        if it == 0:

            def first_update(at):
                value = clamped(at, 0.0 - length * direction[at, :])
                out_ref[at, :] = value
                direction_half[at, :] = value.astype(BF16)

            each_block(first_update)

            def local_term(at):
                value = mul(op_ref[at, :], direction_half[...]) - loads_ref[at, :]
                field[at, :] = value
                high, low = halves(value)
                pieces[at, 0:cases] = high
                pieces[at, cases:] = low

            each_block(local_term)
        else:

            def last_update(at):
                out_ref[at, :] = clamped(at, out_ref[at, :] - length * direction[at, :])

            each_block(last_update)

        for f in range(4):
            if it == 0:
                sent_side(f, mode_send.at[f], mode_recv, mode_sems)
            sent_side(f, product_send.at[it, f], product_recv.at[it], product_sems.at[it])
            sent_side(f, face_send.at[it, f], face_recv.at[it], face_sems.at[it])
            sent_side(f, amount_send.at[it], amount_recv.at[it], amount_sems.at[it])
        for k in range(rows):
            if k == 0:

                @pl.when(jnp.logical_not(at_home))
                def _():
                    coef(0).wait_send()

            else:
                coef(k).wait_send()
        for k in range(1, cols):
            part(k).wait_send()


def per_device(rows, cols, local_ops, loads, modes, coarse_inverse, face_rows, adjacency, contact):
    order, cases = loads.shape[2:]
    mode_count = modes.shape[2]
    face = face_rows.shape[3]
    group = coarse_inverse.shape[1] // mode_count
    stack = 5 * mode_count
    vmem = pl.BlockSpec(memory_space=pltpu.VMEM)
    dma = pltpu.SemaphoreType.DMA
    scratch = [
        pltpu.VMEM((order, order), BF16),
        pltpu.VMEM((order, order), BF16),
        pltpu.VMEM((order, order), BF16),
        pltpu.VMEM((order, 2 * cases), BF16),
        pltpu.VMEM((stack, order), BF16),
        pltpu.VMEM((stack, order), BF16),
        pltpu.VMEM((order, stack), BF16),
        pltpu.VMEM((order, stack), BF16),
        pltpu.VMEM((order, LANES), F32),
        pltpu.VMEM((order, LANES), F32),
        pltpu.VMEM((order, cases), F32),
        pltpu.VMEM((order, cases), F32),
        pltpu.VMEM((order, cases), BF16),
        pltpu.VMEM((4, mode_count, face), F32),
        pltpu.VMEM((4, mode_count, face), F32),
        pltpu.VMEM((ITERS, 4, face, cases), F32),
        pltpu.VMEM((ITERS, 4, face, cases), F32),
        pltpu.VMEM((ITERS, 4, mode_count, cases), F32),
        pltpu.VMEM((ITERS, 4, mode_count, cases), F32),
        pltpu.VMEM((ITERS, mode_count, cases), F32),
        pltpu.VMEM((ITERS, group, mode_count, cases), F32),
        pltpu.VMEM((ITERS, cols, mode_count, cases), F32),
        pltpu.VMEM((ITERS, cols, mode_count, cases), F32),
        pltpu.VMEM((ITERS, mode_count, cases), F32),
        pltpu.VMEM((ITERS, 4, mode_count, cases), F32),
        pltpu.VMEM((ITERS, 8, LANES), F32),
        pltpu.VMEM((ITERS, cols, 8, LANES), F32),
        pltpu.VMEM((ITERS, 8, LANES), F32),
        pltpu.VMEM((ITERS, rows, 8, LANES), F32),
        dma,
        dma((2, 4)),
        dma((ITERS, 2, 4)),
        dma((ITERS, 2, 4)),
        dma((ITERS, 2, max(rows, group))),
        dma((ITERS, 2, cols)),
        dma((ITERS, 2, 4)),
        dma((ITERS, 2, cols)),
        dma((ITERS, 2, rows)),
    ]
    result = pl.pallas_call(
        functools.partial(kernel, rows, cols),
        out_shape=jax.ShapeDtypeStruct((order, cases), F32),
        in_specs=[pl.BlockSpec(memory_space=pltpu.SMEM)]
        + [vmem] * 5
        + [pl.BlockSpec(memory_space=pl.ANY)],
        out_specs=vmem,
        scratch_shapes=scratch,
        compiler_params=pltpu.CompilerParams(
            collective_id=0, has_side_effects=True, vmem_limit_bytes=VMEM_BYTES
        ),
        name="dual_steps",
    )(
        adjacency[0],
        modes[0, 0],
        loads[0, 0],
        coarse_inverse,
        face_rows[0, 0],
        contact[0],
        local_ops[0, 0],
    )
    return result[None, None]


def solution(mesh):
    rows, cols = mesh.shape["row"], mesh.shape["col"]
    return jax.shard_map(
        functools.partial(per_device, rows, cols),
        mesh=mesh,
        in_specs=(
            P("row", "col", None, None),
            P("row", "col", None, None),
            P("row", "col", None, None),
            P("row", "col"),
            P("row", "col", None, None),
            P("row", "col", None),
            P("row", "col", None),
        ),
        out_specs=P("row", "col", None, None),
        check_vma=False,
    )
```

```python
import functools

import jax
import jax.numpy as jnp
from jax import lax
from jax.experimental import pallas as pl
from jax.experimental.pallas import tpu as pltpu
from jax.sharding import PartitionSpec as P

ITERS = 2
F32 = jnp.float32
BF16 = jnp.bfloat16
MESH = pl.DeviceIdType.MESH
LANES = 128
VMEM_BYTES = 63_000_000
TICKS = 8
SCHEDULE = (
    {"faces": (0, 1), "sides": (2,), "products": (3,), "coefs": (4, 5), "parts": (6, 7)},
    {"faces": (0, 1), "coefs": (2, 3), "parts": (4, 5, 6, 7)},
)
LOWEST = float(jnp.finfo(jnp.float32).min)


def halves(value):
    high = value.astype(BF16)
    low = (value - high.astype(F32)).astype(BF16)
    return high, low


def mul(a, b):
    return jnp.dot(a, b, preferred_element_type=F32)


def mul_split(a, b):
    a_high, a_low = a
    b_high, b_low = b
    return mul(a_high, b_high) + (mul(a_high, b_low) + mul(a_low, b_high))


def wide(value):
    return jnp.concatenate([value, value], axis=1)


def by_eight(value):
    return value.reshape(value.shape[0] // 8, 8, value.shape[1]).sum(axis=0)


def kernel(
    rows,
    cols,
    adj_ref,
    modes_ref,
    index_ref,
    contact_ref,
    loads_hbm,
    tile_hbm,
    op_hbm,
    out_hbm,
    loads_ref,
    tile_ref,
    op_ref,
    pick,
    place,
    face_op,
    pieces,
    modes_high,
    modes_low,
    modes_high_t,
    modes_low_t,
    row_weight,
    row_floor,
    first_value,
    field,
    direction,
    direction_half,
    mode_send,
    mode_recv,
    face_send,
    face_recv,
    product_send,
    product_recv,
    coef_send,
    coef_recv,
    part_send,
    pair_recv,
    pair_send,
    part_recv,
    amount_send,
    amount_recv,
    first_send,
    first_recv,
    second_send,
    second_recv,
    local_sems,
    mode_sems,
    face_sems,
    strip_sems,
    product_sems,
    coef_sems,
    pair_sems,
    part_sems,
    amount_sems,
    first_sems,
    second_sems,
):
    row = lax.axis_index("row")
    col = lax.axis_index("col")
    order, cases = loads_ref.shape
    mode_count = modes_ref.shape[0]
    face = index_ref.shape[1]
    group = coef_recv.shape[1]
    step = 512
    blocks = order // step

    loads_copy = pltpu.make_async_copy(loads_hbm, loads_ref, local_sems.at[0])
    tile_copy = pltpu.make_async_copy(tile_hbm, tile_ref, local_sems.at[1])
    op_copy = pltpu.make_async_copy(op_hbm, op_ref, local_sems.at[2])
    loads_copy.start()
    tile_copy.start()
    op_copy.start()

    sides = (
        (row > 0, (row - 1, col)),
        (row < rows - 1, (row + 1, col)),
        (col > 0, (row, col - 1)),
        (col < cols - 1, (row, col + 1)),
    )
    coef_col = (row * cols + col) // group
    coef_slot = lax.rem(col, group)
    source_row = (col * group) // cols
    source_col = lax.rem(col * group, cols)
    at_home = coef_col == col

    barrier = pltpu.get_barrier_semaphore()
    for k in range(1, cols):
        pl.semaphore_signal(
            barrier, inc=1, device_id=(row, lax.rem(col + k, cols)), device_id_type=MESH
        )
    for k in range(1, rows):
        pl.semaphore_signal(
            barrier, inc=1, device_id=(lax.rem(row + k, rows), col), device_id_type=MESH
        )
    for k in range(group):
        is_me = (source_row == row) & (source_col + k == col)

        @pl.when(jnp.logical_not(is_me))
        def _():
            pl.semaphore_signal(
                barrier, inc=1, device_id=(source_row, source_col + k), device_id_type=MESH
            )

    for f in range(4):

        @pl.when(jnp.logical_not(sides[f][0]))
        def _():
            mode_recv[f] = jnp.zeros(mode_recv.shape[1:], F32)
            face_recv[f] = jnp.zeros(face_recv.shape[1:], F32)
            for it in range(ITERS):
                product_recv[it, f] = jnp.zeros(product_recv.shape[2:], F32)
                amount_recv[it, f] = jnp.zeros(amount_recv.shape[2:], F32)

    def side_copy(f, source, target, sems):
        return pltpu.make_async_remote_copy(
            src_ref=source,
            dst_ref=target.at[f ^ 1],
            send_sem=sems.at[0, f],
            recv_sem=sems.at[1, f ^ 1],
            device_id=sides[f][1],
            device_id_type=MESH,
        )

    def start_side(f, source, target, sems):
        @pl.when(sides[f][0])
        def _():
            side_copy(f, source, target, sems).start()

    def wait_side(f, target, sems):
        @pl.when(sides[f][0])
        def _():
            pltpu.make_async_remote_copy(
                src_ref=target.at[f],
                dst_ref=target.at[f],
                send_sem=sems.at[0, f],
                recv_sem=sems.at[1, f],
                device_id=sides[f][1],
                device_id_type=MESH,
            ).wait_recv()

    def sent_side(f, source, target, sems):
        @pl.when(sides[f][0])
        def _():
            side_copy(f, source, target, sems).wait_send()

    def fill_pick(faces):
        for f in faces:
            down = jnp.broadcast_to(index_ref[f : f + 1, :], (LANES, face)).T

            @pl.loop(0, order // LANES)
            def _(i):
                there = lax.broadcasted_iota(jnp.int32, (face, LANES), 1) + i * LANES
                at = pl.ds(pl.multiple_of(i * LANES, LANES), LANES)
                pick[f * face : (f + 1) * face, at] = jnp.where(down == there, 1.0, 0.0).astype(
                    BF16
                )

    def send_modes():
        high, low = halves(modes_ref[...])
        modes_high[0:mode_count] = high
        modes_low[0:mode_count] = low
        both = jnp.concatenate([high, low], axis=0)
        for f in range(4):
            moved = lax.dot_general(
                both,
                pick[f * face : (f + 1) * face, :],
                (((1,), (1,)), ((), ())),
                preferred_element_type=F32,
            )
            mode_send[f] = moved[0:mode_count] + moved[mode_count:]
        for f in range(4):
            start_side(f, mode_send.at[f], mode_recv, mode_sems)

    def greet():
        here = (source_row == row) & (source_col <= col) & (col < source_col + group)
        greeted = cols - 1 + rows - 1 + group - here.astype(jnp.int32)
        pl.semaphore_wait(barrier, greeted)

    def pick_op(f):
        @pl.loop(0, order // step)
        def _(i):
            at = pl.ds(pl.multiple_of(i * step, step), step)
            face_op[f * face : (f + 1) * face, at] = mul(
                pick[f * face : (f + 1) * face, :], op_ref[:, at]
            ).astype(BF16)

    def fill_place():
        @pl.loop(0, order // 256)
        def _(i):
            at = pl.ds(pl.multiple_of(i * 256, 256), 256)
            for f in range(4):
                here = lax.broadcasted_iota(jnp.int32, (256, face), 0) + i * 256
                hit = here == index_ref[f : f + 1, :]
                place[at, f * face : (f + 1) * face] = jnp.where(hit, 1.0, 0.0).astype(BF16)

    def strip(it, f, j, incoming):
        tall = face // TICKS
        at = pl.ds(j * tall, tall)
        if incoming:
            source = face_recv.at[f, at]
            target = source
            arrived = f
        else:
            source = face_send.at[f, at]
            target = face_recv.at[f ^ 1, at]
            arrived = f ^ 1
        return pltpu.make_async_remote_copy(
            src_ref=source,
            dst_ref=target,
            send_sem=strip_sems.at[0, f, j],
            recv_sem=strip_sems.at[1, arrived, j],
            device_id=sides[f][1],
            device_id_type=MESH,
        )

    def tick(it, point):
        for j in SCHEDULE[it].get(point, ()):
            for f in range(2):

                @pl.when(sides[f][0])
                def _():
                    strip(it, f, j, False).start()

    def wait_strips(it, *ticks):
        for j in ticks:
            for f in range(2):

                @pl.when(sides[f][0])
                def _():
                    strip(it, f, j, True).wait_recv()

    def sent_strips(it):
        for j in range(TICKS):
            for f in range(2):

                @pl.when(sides[f][0])
                def _():
                    strip(it, f, j, False).wait_send()

    def each_block(body):
        @pl.loop(0, blocks)
        def _(i):
            body(pl.ds(pl.multiple_of(i * step, step), step))

    def negate(at):
        value = -loads_ref[at, :]
        field[at, :] = value
        high, low = halves(value)
        pieces[at, 0:cases] = high
        pieces[at, cases:] = low

    def faces_of_field(it, faces):
        for f in faces:
            moved = mul(pick[f * face : (f + 1) * face, :], pieces[...])
            face_send[f] = moved[:, 0:cases] + moved[:, cases:]

    def flag(f):
        return adj_ref[0, f].astype(F32)

    def fill_modes():
        for f in range(4):
            high, low = halves(mode_recv[f])
            moved = mul(
                jnp.concatenate([high, low], axis=0), pick[f * face : (f + 1) * face, :]
            )
            high, low = halves(moved[0:mode_count] + moved[mode_count:])
            at = slice((f + 1) * mode_count, (f + 2) * mode_count)
            modes_high[at] = high
            modes_low[at] = low
        modes_high_t[...] = modes_high[...].astype(F32).T.astype(BF16)
        modes_low_t[...] = modes_low[...].astype(F32).T.astype(BF16)

    def fill_rows():
        flags = jnp.concatenate(
            [jnp.full((face, LANES), flag(f), F32) for f in range(4)], axis=0
        ).astype(BF16)
        for i in range(blocks):
            glued = mul(place[i * step : (i + 1) * step, :], flags)
            touching = (
                jnp.broadcast_to(contact_ref[:, i * step : (i + 1) * step], (LANES, step))
                .astype(F32)
                .T
            )
            free = 1.0 - glued
            row_weight[i * step : (i + 1) * step, :] = 0.5 + 0.5 * free
            floor = jnp.where(touching * free > 0.5, 0.0, LOWEST)
            row_floor[i * step : (i + 1) * step, :] = wide(floor)

    def clamped(at, value):
        return jnp.maximum(value, row_floor[at, :])

    def all_sum(it, totals):
        parts = cases // LANES
        tile = jnp.concatenate(
            [totals[t : t + 1, p * LANES : (p + 1) * LANES] for t in range(2) for p in range(parts)]
            + [jnp.zeros((8 - 2 * parts, LANES), F32)],
            axis=0,
        )
        first_send[it] = tile

        def first(k):
            return pltpu.make_async_remote_copy(
                src_ref=first_send.at[it],
                dst_ref=first_recv.at[it, k],
                send_sem=first_sems.at[0, k],
                recv_sem=first_sems.at[1, k],
                device_id=(row, lax.rem(col + k, cols)),
                device_id_type=MESH,
            )

        for k in range(1, cols):
            first(k).start()
        for k in range(1, cols):
            first(k).wait_recv()
        tile = tile + first_recv[it, 1:cols].sum(axis=0)
        second_send[it] = tile

        def second(k):
            return pltpu.make_async_remote_copy(
                src_ref=second_send.at[it],
                dst_ref=second_recv.at[it, k],
                send_sem=second_sems.at[0, k],
                recv_sem=second_sems.at[1, k],
                device_id=(lax.rem(row + k, rows), col),
                device_id_type=MESH,
            )

        for k in range(1, rows):
            second(k).start()
        for k in range(1, rows):
            second(k).wait_recv()
        tile = tile + second_recv[it, 1:rows].sum(axis=0)
        for k in range(1, cols):
            first(k).wait_send()
        for k in range(1, rows):
            second(k).wait_send()
        top = jnp.concatenate([tile[p : p + 1] for p in range(parts)], axis=1)
        low = jnp.concatenate([tile[parts + p : parts + p + 1] for p in range(parts)], axis=1)
        return top / low

    for it in range(ITERS):
        if it == 0:
            fill_pick((0, 1))
            loads_copy.wait()
            each_block(negate)
            faces_of_field(it, (0, 1))
            greet()
            tick(it, "faces")
            fill_pick((2, 3))
            send_modes()
            faces_of_field(it, (2, 3))
            for f in (2, 3):
                start_side(f, face_send.at[f], face_recv, face_sems)
            tick(it, "sides")
            fill_place()
            for f in range(4):
                wait_side(f, mode_recv, mode_sems)
            for f in range(4):
                mode_recv[f] = mode_recv[f] * flag(f)
            for f in range(4):
                product_send[it, f] = mul_split(halves(mode_recv[f]), halves(face_send[f]))
            for f in range(4):
                start_side(f, product_send.at[it, f], product_recv.at[it], product_sems)
            tick(it, "products")
            own = mul_split(
                (modes_high[0:mode_count], modes_low[0:mode_count]),
                (pieces[:, 0:cases], pieces[:, cases:]),
            )
        else:
            products = mul_split(
                (modes_high[...], modes_low[...]), (pieces[:, 0:cases], pieces[:, cases:])
            )
            own = products[0:mode_count]
            for f in range(4):
                product_send[it, f] = products[(f + 1) * mode_count : (f + 2) * mode_count]
            for f in range(4):
                start_side(f, product_send.at[it, f], product_recv.at[it], product_sems)
            tick(it, "products")
            faces_of_field(it, (2, 3))
            for f in (2, 3):
                start_side(f, face_send.at[f], face_recv, face_sems)
            tick(it, "sides")
        for f in range(4):
            wait_side(f, product_recv.at[it], product_sems)
            own = own + product_recv[it, f]
        coef_send[it] = own

        def coef(k):
            return pltpu.make_async_remote_copy(
                src_ref=coef_send.at[it],
                dst_ref=coef_recv.at[it, coef_slot],
                send_sem=coef_sems.at[0, k],
                recv_sem=coef_sems.at[1, coef_slot],
                device_id=(lax.rem(row + k, rows), coef_col),
                device_id_type=MESH,
            )

        for k in range(rows):
            if k == 0:

                @pl.when(at_home)
                def _():
                    coef_recv[it, coef_slot] = own

                @pl.when(jnp.logical_not(at_home))
                def _():
                    coef(0).start()

            else:
                coef(k).start()
        tick(it, "coefs")
        if it == 0:
            fill_modes()
            fill_rows()
            op_copy.wait()
            pick_op(0)
            tile_copy.wait()
        for k in range(group):
            is_me = (source_row == row) & (source_col + k == col)

            @pl.when(jnp.logical_not(is_me))
            def _():
                pltpu.make_async_remote_copy(
                    src_ref=coef_send.at[it],
                    dst_ref=coef_recv.at[it, k],
                    send_sem=coef_sems.at[0, 0],
                    recv_sem=coef_sems.at[1, k],
                    device_id=(source_row, source_col + k),
                    device_id_type=MESH,
                ).wait_recv()

        block = coef_recv[it].reshape(group * mode_count, cases)
        partial = mul_split(halves(tile_ref[...]), halves(block)).reshape(
            cols // 2, 2, mode_count, cases
        )
        part_send[it, 0] = partial[:, 0]
        part_send[it, 1] = partial[:, 1]
        core = lax.rem(col, 2)
        pair = pltpu.make_async_remote_copy(
            src_ref=part_send.at[it, 1 - core],
            dst_ref=pair_recv.at[it],
            send_sem=pair_sems.at[0],
            recv_sem=pair_sems.at[1],
            device_id=(row, col + 1 - 2 * core),
            device_id_type=MESH,
        )
        pair.start()
        pair.wait_recv()
        pair_send[it] = part_send[it, core] + pair_recv[it]

        def part(k):
            target = lax.rem(col + 2 * k, cols)
            return pltpu.make_async_remote_copy(
                src_ref=pair_send.at[it, target // 2],
                dst_ref=part_recv.at[it, k],
                send_sem=part_sems.at[0, k],
                recv_sem=part_sems.at[1, k],
                device_id=(row, target),
                device_id_type=MESH,
            )

        for k in range(1, cols // 2):
            part(k).start()
        def spread(f, at):
            high, low = halves(face_recv[f, at] * flag(f))
            return jnp.concatenate([high, low], axis=1)

        def add_sides():
            for f in (2, 3):
                pieces[f * face : (f + 1) * face, :] = spread(f, slice(0, face))

            def add(at):
                moved = mul(place[at, 2 * face : 4 * face], pieces[2 * face : 4 * face, :])
                field[at, :] = field[at, :] + (moved[:, 0:cases] + moved[:, cases:])

            each_block(add)

        def add_strips(j):
            tall = 2 * (face // TICKS)
            span = slice(j // 2 * tall, (j // 2 + 1) * tall)
            lower = slice(face + j // 2 * tall, face + (j // 2 + 1) * tall)
            wait_strips(it, j, j + 1)
            both = jnp.concatenate([spread(0, span), spread(1, span)], axis=0)

            def add(at):
                there = jnp.concatenate([place[at, span], place[at, lower]], axis=1)
                moved = mul(there, both)
                field[at, :] = field[at, :] + (moved[:, 0:cases] + moved[:, cases:])

            each_block(add)

        tick(it, "parts")
        for f in (2, 3):
            wait_side(f, face_recv, face_sems)
        add_sides()
        for k in range(1, cols // 2):
            part(k).wait_recv()
        amount = pair_send[it, col // 2] + part_recv[it, 1 : cols // 2].sum(axis=0)
        amount_send[it] = amount
        for f in range(4):
            start_side(f, amount_send.at[it], amount_recv.at[it], amount_sems)
        tick(it, "amounts")
        if it == 0:
            pick_op(1)
        for j in range(0, TICKS, 2):
            add_strips(j)
        for f in range(4):
            wait_side(f, amount_recv.at[it], amount_sems)
        amounts = halves(
            jnp.concatenate([amount] + [amount_recv[it, f] for f in range(4)], axis=0)
        )

        def turn(i, total):
            at = pl.ds(pl.multiple_of(i * step, step), step)
            value = field[at, :] - mul_split((modes_high_t[at, :], modes_low_t[at, :]), amounts)
            direction[at, :] = value
            direction_half[at, :] = value.astype(BF16)
            return total + by_eight(wide(row_weight[at, :]) * value * value)

        top = lax.fori_loop(0, blocks, turn, jnp.zeros((8, cases), F32))
        def operate(i, total):
            at = pl.ds(pl.multiple_of(i * step, step), step)
            return total + by_eight(direction[at, :] * mul(op_ref[at, :], direction_half[...]))

        low = lax.fori_loop(0, blocks, operate, jnp.zeros((8, cases), F32))
        totals = jnp.concatenate(
            [top.sum(axis=0, keepdims=True), low.sum(axis=0, keepdims=True)], axis=0
        )
        for f in range(4):
            if it == 0:
                sent_side(f, mode_send.at[f], mode_recv, mode_sems)
            sent_side(f, product_send.at[it, f], product_recv.at[it], product_sems)
            if f >= 2:
                sent_side(f, face_send.at[f], face_recv, face_sems)
            sent_side(f, amount_send.at[it], amount_recv.at[it], amount_sems)
        for k in range(rows):
            if k == 0:

                @pl.when(jnp.logical_not(at_home))
                def _():
                    coef(0).wait_send()

            else:
                coef(k).wait_send()
        for k in range(1, cols // 2):
            part(k).wait_send()
        pair.wait_send()
        sent_strips(it)
        length = all_sum(it, totals)

        if it == 0:

            def first_update(at):
                value = clamped(at, 0.0 - length * direction[at, :])
                first_value[at, :] = value
                direction_half[at, :] = value.astype(BF16)

            each_block(first_update)
            for f in (0, 1):
                face_send[f] = face_send[f] + mul(
                    face_op[f * face : (f + 1) * face, :], direction_half[...]
                )
            tick(it + 1, "faces")

            def local_term(at):
                value = mul(op_ref[at, :], direction_half[...]) - loads_ref[at, :]
                field[at, :] = value
                high, low = halves(value)
                pieces[at, 0:cases] = high
                pieces[at, cases:] = low

            each_block(local_term)
        else:

            def out_copy(i):
                at = slice(i * step, (i + 1) * step)
                return pltpu.make_async_copy(field.at[at], out_hbm.at[at], local_sems.at[3 + i])

            for i in range(blocks):
                at = slice(i * step, (i + 1) * step)
                field[at, :] = clamped(at, first_value[at, :] - length * direction[at, :])
                out_copy(i).start()

    for i in range(blocks):
        out_copy(i).wait()


def per_device(rows, cols, local_ops, loads, modes, coarse_inverse, face_rows, adjacency, contact):
    order, cases = loads.shape[2:]
    mode_count = modes.shape[2]
    face = face_rows.shape[3]
    group = coarse_inverse.shape[1] // mode_count
    stack = 5 * mode_count
    vmem = pl.BlockSpec(memory_space=pltpu.VMEM)
    dma = pltpu.SemaphoreType.DMA
    scratch = [
        pltpu.VMEM((order, cases), F32),
        pltpu.VMEM(coarse_inverse.shape, F32),
        pltpu.VMEM((order, order), BF16),
        pltpu.VMEM((order, order), BF16),
        pltpu.VMEM((order, order), BF16),
        pltpu.VMEM((2 * face, order), BF16),
        pltpu.VMEM((order, 2 * cases), BF16),
        pltpu.VMEM((stack, order), BF16),
        pltpu.VMEM((stack, order), BF16),
        pltpu.VMEM((order, stack), BF16),
        pltpu.VMEM((order, stack), BF16),
        pltpu.VMEM((order, LANES), F32),
        pltpu.VMEM((order, cases), F32),
        pltpu.VMEM((order, cases), F32),
        pltpu.VMEM((order, cases), F32),
        pltpu.VMEM((order, cases), F32),
        pltpu.VMEM((order, cases), BF16),
        pltpu.VMEM((4, mode_count, face), F32),
        pltpu.VMEM((4, mode_count, face), F32),
        pltpu.VMEM((4, face, cases), F32),
        pltpu.VMEM((4, face, cases), F32),
        pltpu.VMEM((ITERS, 4, mode_count, cases), F32),
        pltpu.VMEM((ITERS, 4, mode_count, cases), F32),
        pltpu.VMEM((ITERS, mode_count, cases), F32),
        pltpu.VMEM((ITERS, group, mode_count, cases), F32),
        pltpu.VMEM((ITERS, 2, cols // 2, mode_count, cases), F32),
        pltpu.VMEM((ITERS, cols // 2, mode_count, cases), F32),
        pltpu.VMEM((ITERS, cols // 2, mode_count, cases), F32),
        pltpu.VMEM((ITERS, cols // 2, mode_count, cases), F32),
        pltpu.VMEM((ITERS, mode_count, cases), F32),
        pltpu.VMEM((ITERS, 4, mode_count, cases), F32),
        pltpu.VMEM((ITERS, 8, LANES), F32),
        pltpu.VMEM((ITERS, cols, 8, LANES), F32),
        pltpu.VMEM((ITERS, 8, LANES), F32),
        pltpu.VMEM((ITERS, rows, 8, LANES), F32),
        dma((3 + 4,)),
        dma((2, 4)),
        dma((2, 4)),
        dma((2, 2, TICKS)),
        dma((2, 4)),
        dma((2, max(rows, group))),
        dma((2,)),
        dma((2, cols // 2)),
        dma((2, 4)),
        dma((2, cols)),
        dma((2, rows)),
    ]
    anywhere = pl.BlockSpec(memory_space=pl.ANY)
    result = pl.pallas_call(
        functools.partial(kernel, rows, cols),
        out_shape=jax.ShapeDtypeStruct((order, cases), F32),
        in_specs=[pl.BlockSpec(memory_space=pltpu.SMEM)]
        + [vmem] * 3
        + [anywhere] * 3,
        out_specs=anywhere,
        scratch_shapes=scratch,
        compiler_params=pltpu.CompilerParams(
            collective_id=0, has_side_effects=True, vmem_limit_bytes=VMEM_BYTES
        ),
        name="dual_steps",
    )(
        adjacency[0],
        modes[0, 0],
        face_rows[0, 0],
        contact[0],
        loads[0, 0],
        coarse_inverse,
        local_ops[0, 0],
    )
    return result[None, None]


def solution(mesh):
    rows, cols = mesh.shape["row"], mesh.shape["col"]
    return jax.shard_map(
        functools.partial(per_device, rows, cols),
        mesh=mesh,
        in_specs=(
            P("row", "col", None, None),
            P("row", "col", None, None),
            P("row", "col", None, None),
            P("row", "col"),
            P("row", "col", None, None),
            P("row", "col", None),
            P("row", "col", None),
        ),
        out_specs=P("row", "col", None, None),
        check_vma=False,
    )
```

```python
import functools

import jax
import jax.numpy as jnp
from jax import lax
from jax.experimental import pallas as pl
from jax.experimental.pallas import tpu as pltpu
from jax.sharding import PartitionSpec as P

ITERS = 2
F32 = jnp.float32
BF16 = jnp.bfloat16
MESH = pl.DeviceIdType.MESH
LANES = 128
VMEM_BYTES = 63_000_000
TICKS = 8
SCHEDULE = (
    {"faces": (0,), "products": (1,), "coefs": (2, 3, 4), "parts": (5, 6), "amounts": (7,)},
    {"faces": (0, 1), "parts": (2, 3, 4), "amounts": (5, 6, 7)},
)
AHEAD = 2
LOWEST = float(jnp.finfo(jnp.float32).min)
EARLY = (4, 0)


def halves(value):
    high = value.astype(BF16)
    low = (value - high.astype(F32)).astype(BF16)
    return high, low


def mul(a, b):
    return jnp.dot(a, b, preferred_element_type=F32)


def mul_split(a, b):
    a_high, a_low = a
    b_high, b_low = b
    return mul(a_high, b_high) + (mul(a_high, b_low) + mul(a_low, b_high))


def wide(value):
    return jnp.concatenate([value, value], axis=1)


def by_eight(value):
    return value.reshape(value.shape[0] // 8, 8, value.shape[1]).sum(axis=0)


def kernel(
    rows,
    cols,
    adj_ref,
    modes_ref,
    index_ref,
    contact_ref,
    loads_hbm,
    tile_hbm,
    op_hbm,
    out_hbm,
    loads_ref,
    tile_ref,
    op_ref,
    pick,
    place,
    face_op,
    mode_op_high,
    mode_op_low,
    first_own,
    pieces,
    modes_high,
    modes_low,
    modes_high_t,
    modes_low_t,
    row_weight,
    row_floor,
    first_value,
    field,
    direction,
    direction_half,
    mode_send,
    mode_recv,
    face_send,
    face_recv,
    passing,
    product_send,
    product_recv,
    coef_send,
    coef_recv,
    part_send,
    pair_recv,
    pair_send,
    part_recv,
    amount_send,
    amount_recv,
    first_send,
    first_recv,
    second_send,
    second_recv,
    local_sems,
    mode_sems,
    face_sems,
    pass_sems,
    strip_sems,
    product_sems,
    coef_sems,
    pair_sems,
    part_sems,
    amount_sems,
    first_sems,
    second_sems,
):
    row = lax.axis_index("row")
    col = lax.axis_index("col")
    order, cases = loads_ref.shape
    mode_count = modes_ref.shape[0]
    face = index_ref.shape[1]
    group = coef_recv.shape[1]
    step = 512
    blocks = order // step
    ahead = AHEAD * (face // TICKS)

    loads_copy = pltpu.make_async_copy(loads_hbm, loads_ref, local_sems.at[0])
    tile_copy = pltpu.make_async_copy(tile_hbm, tile_ref, local_sems.at[1])
    op_copy = pltpu.make_async_copy(op_hbm, op_ref, local_sems.at[2])
    loads_copy.start()
    tile_copy.start()
    op_copy.start()

    sides = (
        (row > 0, (row - 1, col)),
        (row < rows - 1, (row + 1, col)),
        (col > 0, (row, col - 1)),
        (col < cols - 1, (row, col + 1)),
    )
    coef_col = (row * cols + col) // group
    coef_slot = lax.rem(col, group)
    source_row = (col * group) // cols
    source_col = lax.rem(col * group, cols)
    at_home = coef_col == col

    barrier = pltpu.get_barrier_semaphore()
    for k in range(1, cols):
        pl.semaphore_signal(
            barrier, inc=1, device_id=(row, lax.rem(col + k, cols)), device_id_type=MESH
        )
    for k in range(1, rows):
        pl.semaphore_signal(
            barrier, inc=1, device_id=(lax.rem(row + k, rows), col), device_id_type=MESH
        )
    for k in range(group):
        is_me = (source_row == row) & (source_col + k == col)

        @pl.when(jnp.logical_not(is_me))
        def _():
            pl.semaphore_signal(
                barrier, inc=1, device_id=(source_row, source_col + k), device_id_type=MESH
            )

    for f in range(4):

        @pl.when(jnp.logical_not(sides[f][0]))
        def _():
            mode_recv[f] = jnp.zeros(mode_recv.shape[1:], F32)
            face_recv[f] = jnp.zeros(face_recv.shape[1:], F32)
            for it in range(ITERS):
                product_recv[it, f] = jnp.zeros(product_recv.shape[2:], F32)
                amount_recv[it, f] = jnp.zeros(amount_recv.shape[2:], F32)

    def side_copy(f, source, target, sems):
        return pltpu.make_async_remote_copy(
            src_ref=source,
            dst_ref=target.at[f ^ 1],
            send_sem=sems.at[0, f],
            recv_sem=sems.at[1, f ^ 1],
            device_id=sides[f][1],
            device_id_type=MESH,
        )

    def start_side(f, source, target, sems):
        @pl.when(sides[f][0])
        def _():
            side_copy(f, source, target, sems).start()

    def wait_side(f, target, sems):
        @pl.when(sides[f][0])
        def _():
            pltpu.make_async_remote_copy(
                src_ref=target.at[f],
                dst_ref=target.at[f],
                send_sem=sems.at[0, f],
                recv_sem=sems.at[1, f],
                device_id=sides[f][1],
                device_id_type=MESH,
            ).wait_recv()

    def sent_side(f, source, target, sems):
        @pl.when(sides[f][0])
        def _():
            side_copy(f, source, target, sems).wait_send()

    def fill_pick(faces):
        for f in faces:
            down = jnp.broadcast_to(index_ref[f : f + 1, :], (LANES, face)).T

            @pl.loop(0, order // LANES)
            def _(i):
                there = lax.broadcasted_iota(jnp.int32, (face, LANES), 1) + i * LANES
                at = pl.ds(pl.multiple_of(i * LANES, LANES), LANES)
                pick[f * face : (f + 1) * face, at] = jnp.where(down == there, 1.0, 0.0).astype(
                    BF16
                )

    def make_modes():
        high, low = halves(modes_ref[...])
        modes_high[0:mode_count] = high
        modes_low[0:mode_count] = low
        both = jnp.concatenate([high, low], axis=0)
        for f in range(4):
            moved = lax.dot_general(
                both,
                pick[f * face : (f + 1) * face, :],
                (((1,), (1,)), ((), ())),
                preferred_element_type=F32,
            )
            mode_send[f] = moved[0:mode_count] + moved[mode_count:]

    def greet():
        here = (source_row == row) & (source_col <= col) & (col < source_col + group)
        greeted = cols - 1 + rows - 1 + group - here.astype(jnp.int32)
        pl.semaphore_wait(barrier, greeted)

    def modes_op():
        both = jnp.concatenate([modes_high[...], modes_low[...]], axis=0)
        count = modes_high.shape[0]

        @pl.loop(0, order // step)
        def _(i):
            at = pl.ds(pl.multiple_of(i * step, step), step)
            moved = mul(both, op_ref[:, at])
            high, low = halves(moved[0:count] + moved[count:])
            mode_op_high[:, at] = high
            mode_op_low[:, at] = low

    def pick_op():
        both = jnp.concatenate([pick[0:ahead, :], pick[face : face + ahead, :]], axis=0)

        @pl.loop(0, order // step)
        def _(i):
            at = pl.ds(pl.multiple_of(i * step, step), step)
            face_op[:, at] = mul(both, op_ref[:, at]).astype(BF16)

    def fill_place():
        @pl.loop(0, order // 256)
        def _(i):
            at = pl.ds(pl.multiple_of(i * 256, 256), 256)
            for f in range(4):
                here = lax.broadcasted_iota(jnp.int32, (256, face), 0) + i * 256
                hit = here == index_ref[f : f + 1, :]
                place[at, f * face : (f + 1) * face] = jnp.where(hit, 1.0, 0.0).astype(BF16)

    seam = cols // 2
    crossing = {2: col == seam, 3: col == seam - 1}
    over = {2: 1, 3: cols - 2}
    short = face // 2

    def lateral(f, part, incoming):
        at = pl.ds(part * short, short)
        return pltpu.make_async_remote_copy(
            src_ref=face_recv.at[f, at] if incoming else face_send.at[f, at],
            dst_ref=face_recv.at[f if incoming else f ^ 1, at],
            send_sem=face_sems.at[0, f, part],
            recv_sem=face_sems.at[1, f if incoming else f ^ 1, part],
            device_id=sides[f][1],
            device_id_type=MESH,
        )

    def detour(f):
        return pltpu.make_async_remote_copy(
            src_ref=face_send.at[f, pl.ds(short, short)],
            dst_ref=passing,
            send_sem=face_sems.at[0, f, 1],
            recv_sem=pass_sems.at[0],
            device_id=(row, over[f]),
            device_id_type=MESH,
        )

    def onward(f):
        return pltpu.make_async_remote_copy(
            src_ref=passing,
            dst_ref=face_recv.at[f ^ 1, pl.ds(short, short)],
            send_sem=pass_sems.at[1],
            recv_sem=face_sems.at[1, f ^ 1, 1],
            device_id=(row, seam - 1 if f == 2 else seam),
            device_id_type=MESH,
        )

    def start_lateral(f):
        @pl.when(sides[f][0])
        def _():
            lateral(f, 0, False).start()

        @pl.when(sides[f][0] & jnp.logical_not(crossing[f]))
        def _():
            lateral(f, 1, False).start()

        @pl.when(crossing[f])
        def _():
            detour(f).start()

    def pass_lateral():
        for f in (2, 3):

            @pl.when(col == over[f])
            def _():
                detour(f).wait_recv()
                onward(f).start()

    def wait_lateral(f):
        for part in range(2):

            @pl.when(sides[f][0])
            def _():
                lateral(f, part, True).wait_recv()

    def sent_lateral(f):
        for part in range(2):

            @pl.when(sides[f][0])
            def _():
                lateral(f, part, False).wait_send()

        @pl.when(col == over[f])
        def _():
            onward(f).wait_send()

    def strip(it, f, j, incoming):
        tall = face // TICKS
        at = pl.ds(j * tall, tall)
        if incoming:
            source = face_recv.at[f, at]
            target = source
            arrived = f
        else:
            source = face_send.at[f, at]
            target = face_recv.at[f ^ 1, at]
            arrived = f ^ 1
        return pltpu.make_async_remote_copy(
            src_ref=source,
            dst_ref=target,
            send_sem=strip_sems.at[0, f, j],
            recv_sem=strip_sems.at[1, arrived, j],
            device_id=sides[f][1],
            device_id_type=MESH,
        )

    def tick(it, point):
        for j in SCHEDULE[it].get(point, ()):
            for f in range(2):

                @pl.when(sides[f][0])
                def _():
                    strip(it, f, j, False).start()

    def wait_strips(it, *ticks):
        for j in ticks:
            for f in range(2):

                @pl.when(sides[f][0])
                def _():
                    strip(it, f, j, True).wait_recv()

    def sent_strips(it):
        for j in range(TICKS):
            for f in range(2):

                @pl.when(sides[f][0])
                def _():
                    strip(it, f, j, False).wait_send()

    def each_block(body):
        @pl.loop(0, blocks)
        def _(i):
            body(pl.ds(pl.multiple_of(i * step, step), step))

    def negate(at):
        value = -loads_ref[at, :]
        field[at, :] = value
        high, low = halves(value)
        pieces[at, 0:cases] = high
        pieces[at, cases:] = low

    def faces_of_field(it, faces):
        for f in faces:
            moved = mul(pick[f * face : (f + 1) * face, :], pieces[...])
            face_send[f] = moved[:, 0:cases] + moved[:, cases:]

    def flag(f):
        return adj_ref[0, f].astype(F32)

    def fill_modes():
        for f in range(4):
            high, low = halves(mode_recv[f])
            moved = mul(
                jnp.concatenate([high, low], axis=0), pick[f * face : (f + 1) * face, :]
            )
            high, low = halves(moved[0:mode_count] + moved[mode_count:])
            at = slice((f + 1) * mode_count, (f + 2) * mode_count)
            modes_high[at] = high
            modes_low[at] = low
        modes_high_t[...] = modes_high[...].astype(F32).T.astype(BF16)
        modes_low_t[...] = modes_low[...].astype(F32).T.astype(BF16)

    def fill_rows():
        flags = jnp.concatenate(
            [jnp.full((face, LANES), flag(f), F32) for f in range(4)], axis=0
        ).astype(BF16)
        for i in range(blocks):
            glued = mul(place[i * step : (i + 1) * step, :], flags)
            touching = (
                jnp.broadcast_to(contact_ref[:, i * step : (i + 1) * step], (LANES, step))
                .astype(F32)
                .T
            )
            free = 1.0 - glued
            row_weight[i * step : (i + 1) * step, :] = 0.5 + 0.5 * free
            floor = jnp.where(touching * free > 0.5, 0.0, LOWEST)
            row_floor[i * step : (i + 1) * step, :] = floor

    def clamped(at, value):
        return jnp.maximum(value, wide(row_floor[at, :]))

    def all_sum(it, totals):
        parts = cases // LANES
        tile = jnp.concatenate(
            [totals[t : t + 1, p * LANES : (p + 1) * LANES] for t in range(2) for p in range(parts)]
            + [jnp.zeros((8 - 2 * parts, LANES), F32)],
            axis=0,
        )
        first_send[it] = tile

        def first(k):
            return pltpu.make_async_remote_copy(
                src_ref=first_send.at[it],
                dst_ref=first_recv.at[it, k],
                send_sem=first_sems.at[0, k],
                recv_sem=first_sems.at[1, k],
                device_id=(row, lax.rem(col + k, cols)),
                device_id_type=MESH,
            )

        for k in range(1, cols):
            first(k).start()
        for k in range(1, cols):
            first(k).wait_recv()
        tile = tile + first_recv[it, 1:cols].sum(axis=0)
        second_send[it] = tile

        def second(k):
            return pltpu.make_async_remote_copy(
                src_ref=second_send.at[it],
                dst_ref=second_recv.at[it, k],
                send_sem=second_sems.at[0, k],
                recv_sem=second_sems.at[1, k],
                device_id=(lax.rem(row + k, rows), col),
                device_id_type=MESH,
            )

        for k in range(1, rows):
            second(k).start()
        for k in range(1, rows):
            second(k).wait_recv()
        tile = tile + second_recv[it, 1:rows].sum(axis=0)
        for k in range(1, cols):
            first(k).wait_send()
        for k in range(1, rows):
            second(k).wait_send()
        top = jnp.concatenate([tile[p : p + 1] for p in range(parts)], axis=1)
        low = jnp.concatenate([tile[parts + p : parts + p + 1] for p in range(parts)], axis=1)
        return top / low

    for it in range(ITERS):
        if it == 0:
            fill_pick((0, 1, 2, 3))
            make_modes()
            greet()
            for f in range(4):
                start_side(f, mode_send.at[f], mode_recv, mode_sems)
            loads_copy.wait()
            each_block(negate)
            faces_of_field(it, (0, 1))
            tick(it, "faces")
            faces_of_field(it, (2, 3))
            for f in range(4):
                wait_side(f, mode_recv, mode_sems)
            for f in range(4):
                mode_recv[f] = mode_recv[f] * flag(f)
            for f in range(4):
                product_send[it, f] = mul_split(halves(mode_recv[f]), halves(face_send[f]))
            for f in range(4):
                start_side(f, product_send.at[it, f], product_recv.at[it], product_sems)
            tick(it, "products")
            for f in (2, 3):
                start_lateral(f)
            fill_place()
            own = mul_split(
                (modes_high[0:mode_count], modes_low[0:mode_count]),
                (pieces[:, 0:cases], pieces[:, cases:]),
            )
            first_own[...] = own
        else:
            own = next_own
        for f in range(4):
            wait_side(f, product_recv.at[it], product_sems)
            own = own + product_recv[it, f]
        coef_send[it] = own

        def coef(k):
            return pltpu.make_async_remote_copy(
                src_ref=coef_send.at[it],
                dst_ref=coef_recv.at[it, coef_slot],
                send_sem=coef_sems.at[0, k],
                recv_sem=coef_sems.at[1, coef_slot],
                device_id=(lax.rem(row + k, rows), coef_col),
                device_id_type=MESH,
            )

        for k in range(rows):
            if k == 0:

                @pl.when(at_home)
                def _():
                    coef_recv[it, coef_slot] = own

                @pl.when(jnp.logical_not(at_home))
                def _():
                    coef(0).start()

            else:
                coef(k).start()
        tick(it, "coefs")
        if it == 1:
            faces_of_field(it, (2, 3))
            for f in (2, 3):
                start_lateral(f)
        if it == 0:
            fill_modes()
            fill_rows()
            op_copy.wait()
            pick_op()
            modes_op()
            tile_copy.wait()
        for k in range(group):
            is_me = (source_row == row) & (source_col + k == col)

            @pl.when(jnp.logical_not(is_me))
            def _():
                pltpu.make_async_remote_copy(
                    src_ref=coef_send.at[it],
                    dst_ref=coef_recv.at[it, k],
                    send_sem=coef_sems.at[0, 0],
                    recv_sem=coef_sems.at[1, k],
                    device_id=(source_row, source_col + k),
                    device_id_type=MESH,
                ).wait_recv()

        block = coef_recv[it].reshape(group * mode_count, cases)
        partial = mul_split(halves(tile_ref[...]), halves(block)).reshape(
            cols // 2, 2, mode_count, cases
        )
        part_send[it, 0] = partial[:, 0]
        part_send[it, 1] = partial[:, 1]
        core = lax.rem(col, 2)
        pair = pltpu.make_async_remote_copy(
            src_ref=part_send.at[it, 1 - core],
            dst_ref=pair_recv.at[it],
            send_sem=pair_sems.at[0],
            recv_sem=pair_sems.at[1],
            device_id=(row, col + 1 - 2 * core),
            device_id_type=MESH,
        )
        pair.start()
        pair.wait_recv()
        pair_send[it] = part_send[it, core] + pair_recv[it]

        def part(k):
            target = lax.rem(col + 2 * k, cols)
            return pltpu.make_async_remote_copy(
                src_ref=pair_send.at[it, target // 2],
                dst_ref=part_recv.at[it, k],
                send_sem=part_sems.at[0, k],
                recv_sem=part_sems.at[1, k],
                device_id=(row, target),
                device_id_type=MESH,
            )

        for k in range(1, cols // 2):
            part(k).start()
        def spread(f, at):
            high, low = halves(face_recv[f, at] * flag(f))
            return jnp.concatenate([high, low], axis=1)

        def add_sides():
            for f in (2, 3):
                pieces[f * face : (f + 1) * face, :] = spread(f, slice(0, face))

            def add(at):
                moved = mul(place[at, 2 * face : 4 * face], pieces[2 * face : 4 * face, :])
                field[at, :] = field[at, :] + (moved[:, 0:cases] + moved[:, cases:])

            each_block(add)

        def strips(j):
            tall = 2 * (face // TICKS)
            span = slice(j // 2 * tall, (j // 2 + 1) * tall)
            lower = slice(face + j // 2 * tall, face + (j // 2 + 1) * tall)
            wait_strips(it, j, j + 1)
            return span, lower, jnp.concatenate([spread(0, span), spread(1, span)], axis=0)

        def add_strips(j):
            span, lower, both = strips(j)

            def add(at):
                there = jnp.concatenate([place[at, span], place[at, lower]], axis=1)
                moved = mul(there, both)
                field[at, :] = field[at, :] + (moved[:, 0:cases] + moved[:, cases:])

            each_block(add)

        tick(it, "parts")
        pass_lateral()
        for j in range(0, EARLY[it], 2):
            add_strips(j)
        for k in range(1, cols // 2):
            part(k).wait_recv()
        amount = pair_send[it, col // 2] + part_recv[it, 1 : cols // 2].sum(axis=0)
        amount_send[it] = amount
        for f in range(4):
            start_side(f, amount_send.at[it], amount_recv.at[it], amount_sems)
        tick(it, "amounts")
        for f in (2, 3):
            wait_lateral(f)
        add_sides()
        for j in range(EARLY[it], TICKS - 2, 2):
            add_strips(j)
        for f in range(4):
            wait_side(f, amount_recv.at[it], amount_sems)
        amounts = halves(
            jnp.concatenate([amount] + [amount_recv[it, f] for f in range(4)], axis=0)
        )

        def correct(at):
            field[at, :] = field[at, :] - mul_split(
                (modes_high_t[at, :], modes_low_t[at, :]), amounts
            )

        each_block(correct)
        last, lower, both = strips(TICKS - 2)

        def turn(i, total):
            at = pl.ds(pl.multiple_of(i * step, step), step)
            there = jnp.concatenate([place[at, last], place[at, lower]], axis=1)
            moved = mul(there, both)
            value = field[at, :] + (moved[:, 0:cases] + moved[:, cases:])
            direction[at, :] = value
            direction_half[at, :] = value.astype(BF16)
            return total + by_eight(wide(row_weight[at, :]) * value * value)

        top = lax.fori_loop(0, blocks, turn, jnp.zeros((8, cases), F32))
        def operate(i, total):
            at = pl.ds(pl.multiple_of(i * step, step), step)
            return total + by_eight(direction[at, :] * mul(op_ref[at, :], direction_half[...]))

        low = lax.fori_loop(0, blocks, operate, jnp.zeros((8, cases), F32))
        totals = jnp.concatenate(
            [top.sum(axis=0, keepdims=True), low.sum(axis=0, keepdims=True)], axis=0
        )
        for f in range(4):
            if it == 0:
                sent_side(f, mode_send.at[f], mode_recv, mode_sems)
            sent_side(f, product_send.at[it, f], product_recv.at[it], product_sems)
            if f >= 2:
                sent_lateral(f)
            sent_side(f, amount_send.at[it], amount_recv.at[it], amount_sems)
        for k in range(rows):
            if k == 0:

                @pl.when(jnp.logical_not(at_home))
                def _():
                    coef(0).wait_send()

            else:
                coef(k).wait_send()
        for k in range(1, cols // 2):
            part(k).wait_send()
        pair.wait_send()
        sent_strips(it)
        length = all_sum(it, totals)

        if it == 0:

            def first_update(at):
                value = clamped(at, 0.0 - length * direction[at, :])
                first_value[at, :] = value
                direction_half[at, :] = value.astype(BF16)

            each_block(first_update)
            products = mul(mode_op_high[...], direction_half[...]) + mul(
                mode_op_low[...], direction_half[...]
            )
            next_own = products[0:mode_count] + first_own[...]
            for f in range(4):
                at = slice((f + 1) * mode_count, (f + 2) * mode_count)
                product_send[it + 1, f] = products[at] + product_send[it, f]
            for f in range(4):
                start_side(f, product_send.at[it + 1, f], product_recv.at[it + 1], product_sems)
            moved = mul(face_op[...], direction_half[...])
            for f in (0, 1):
                face_send[f, 0:ahead] = face_send[f, 0:ahead] + moved[f * ahead : (f + 1) * ahead]
            tick(it + 1, "faces")

            def local_term(at):
                value = mul(op_ref[at, :], direction_half[...]) - loads_ref[at, :]
                field[at, :] = value
                high, low = halves(value)
                pieces[at, 0:cases] = high
                pieces[at, cases:] = low

            each_block(local_term)
            for f in (0, 1):
                moved = mul(pick[f * face + ahead : (f + 1) * face, :], pieces[...])
                face_send[f, ahead:] = moved[:, 0:cases] + moved[:, cases:]
            tick(it + 1, "sides")
        else:

            def out_copy(i):
                at = slice(i * step, (i + 1) * step)
                return pltpu.make_async_copy(field.at[at], out_hbm.at[at], local_sems.at[3 + i])

            for i in range(blocks):
                at = slice(i * step, (i + 1) * step)
                field[at, :] = clamped(at, first_value[at, :] - length * direction[at, :])
                out_copy(i).start()

    for i in range(blocks):
        out_copy(i).wait()


def per_device(rows, cols, local_ops, loads, modes, coarse_inverse, face_rows, adjacency, contact):
    order, cases = loads.shape[2:]
    mode_count = modes.shape[2]
    face = face_rows.shape[3]
    group = coarse_inverse.shape[1] // mode_count
    stack = 5 * mode_count
    vmem = pl.BlockSpec(memory_space=pltpu.VMEM)
    dma = pltpu.SemaphoreType.DMA
    scratch = [
        pltpu.VMEM((order, cases), F32),
        pltpu.VMEM(coarse_inverse.shape, F32),
        pltpu.VMEM((order, order), BF16),
        pltpu.VMEM((order, order), BF16),
        pltpu.VMEM((order, order), BF16),
        pltpu.VMEM((2 * AHEAD * (face // TICKS), order), BF16),
        pltpu.VMEM((stack, order), BF16),
        pltpu.VMEM((stack, order), BF16),
        pltpu.VMEM((mode_count, cases), F32),
        pltpu.VMEM((order, 2 * cases), BF16),
        pltpu.VMEM((stack, order), BF16),
        pltpu.VMEM((stack, order), BF16),
        pltpu.VMEM((order, stack), BF16),
        pltpu.VMEM((order, stack), BF16),
        pltpu.VMEM((order, LANES), F32),
        pltpu.VMEM((order, LANES), F32),
        pltpu.VMEM((order, cases), F32),
        pltpu.VMEM((order, cases), F32),
        pltpu.VMEM((order, cases), F32),
        pltpu.VMEM((order, cases), BF16),
        pltpu.VMEM((4, mode_count, face), F32),
        pltpu.VMEM((4, mode_count, face), F32),
        pltpu.VMEM((4, face, cases), F32),
        pltpu.VMEM((4, face, cases), F32),
        pltpu.VMEM((face // 2, cases), F32),
        pltpu.VMEM((ITERS, 4, mode_count, cases), F32),
        pltpu.VMEM((ITERS, 4, mode_count, cases), F32),
        pltpu.VMEM((ITERS, mode_count, cases), F32),
        pltpu.VMEM((ITERS, group, mode_count, cases), F32),
        pltpu.VMEM((ITERS, 2, cols // 2, mode_count, cases), F32),
        pltpu.VMEM((ITERS, cols // 2, mode_count, cases), F32),
        pltpu.VMEM((ITERS, cols // 2, mode_count, cases), F32),
        pltpu.VMEM((ITERS, cols // 2, mode_count, cases), F32),
        pltpu.VMEM((ITERS, mode_count, cases), F32),
        pltpu.VMEM((ITERS, 4, mode_count, cases), F32),
        pltpu.VMEM((ITERS, 8, LANES), F32),
        pltpu.VMEM((ITERS, cols, 8, LANES), F32),
        pltpu.VMEM((ITERS, 8, LANES), F32),
        pltpu.VMEM((ITERS, rows, 8, LANES), F32),
        dma((3 + 4,)),
        dma((2, 4)),
        dma((2, 4, 2)),
        dma((2,)),
        dma((2, 2, TICKS)),
        dma((2, 4)),
        dma((2, max(rows, group))),
        dma((2,)),
        dma((2, cols // 2)),
        dma((2, 4)),
        dma((2, cols)),
        dma((2, rows)),
    ]
    anywhere = pl.BlockSpec(memory_space=pl.ANY)
    result = pl.pallas_call(
        functools.partial(kernel, rows, cols),
        out_shape=jax.ShapeDtypeStruct((order, cases), F32),
        in_specs=[pl.BlockSpec(memory_space=pltpu.SMEM)]
        + [vmem] * 3
        + [anywhere] * 3,
        out_specs=anywhere,
        scratch_shapes=scratch,
        compiler_params=pltpu.CompilerParams(
            collective_id=0, has_side_effects=True, vmem_limit_bytes=VMEM_BYTES
        ),
        name="dual_steps",
    )(
        adjacency[0],
        modes[0, 0],
        face_rows[0, 0],
        contact[0],
        loads[0, 0],
        coarse_inverse,
        local_ops[0, 0],
    )
    return result[None, None]


def solution(mesh):
    rows, cols = mesh.shape["row"], mesh.shape["col"]
    return jax.shard_map(
        functools.partial(per_device, rows, cols),
        mesh=mesh,
        in_specs=(
            P("row", "col", None, None),
            P("row", "col", None, None),
            P("row", "col", None, None),
            P("row", "col"),
            P("row", "col", None, None),
            P("row", "col", None),
            P("row", "col", None),
        ),
        out_specs=P("row", "col", None, None),
        check_vma=False,
    )
```

```python
import functools

import jax
import jax.numpy as jnp
from jax import lax
from jax.experimental import pallas as pl
from jax.experimental.pallas import tpu as pltpu
from jax.sharding import PartitionSpec as P

ITERS = 2
F32 = jnp.float32
BF16 = jnp.bfloat16
MESH = pl.DeviceIdType.MESH
LANES = 128
VMEM_BYTES = 63_000_000
TICKS = 8
SCHEDULE = (
    {"faces": (0,), "products": (1,), "coefs": (2, 3), "parts": (4, 5, 6), "amounts": (7,)},
    {"faces": (0, 1), "fill": (2,), "parts": (3, 4, 5), "amounts": (6, 7)},
)
AHEAD = 2
LOWEST = float(jnp.finfo(jnp.float32).min)
EARLY = (4, 0)


def halves(value):
    high = value.astype(BF16)
    low = (value - high.astype(F32)).astype(BF16)
    return high, low


def mul(a, b):
    return jnp.dot(a, b, preferred_element_type=F32)


def mul_split(a, b):
    a_high, a_low = a
    b_high, b_low = b
    return mul(a_high, b_high) + (mul(a_high, b_low) + mul(a_low, b_high))


def wide(value):
    return jnp.concatenate([value, value], axis=1)


def by_eight(value):
    return value.reshape(value.shape[0] // 8, 8, value.shape[1]).sum(axis=0)


def kernel(
    rows,
    cols,
    adj_ref,
    modes_ref,
    index_ref,
    contact_ref,
    loads_hbm,
    tile_hbm,
    op_hbm,
    out_hbm,
    loads_ref,
    tile_ref,
    op_ref,
    pick,
    place,
    face_op,
    mode_op_high,
    mode_op_low,
    first_own,
    pieces,
    modes_high,
    modes_low,
    modes_high_t,
    modes_low_t,
    row_weight,
    row_floor,
    first_value,
    field,
    direction,
    direction_half,
    mode_send,
    mode_recv,
    face_send,
    face_recv,
    passing,
    product_send,
    product_recv,
    coef_send,
    coef_recv,
    part_send,
    pair_recv,
    pair_send,
    part_recv,
    amount_send,
    amount_recv,
    first_send,
    first_recv,
    second_send,
    second_recv,
    local_sems,
    mode_sems,
    face_sems,
    pass_sems,
    strip_sems,
    product_sems,
    coef_sems,
    pair_sems,
    part_sems,
    amount_sems,
    first_sems,
    second_sems,
):
    row = lax.axis_index("row")
    col = lax.axis_index("col")
    order, cases = loads_ref.shape
    mode_count = modes_ref.shape[0]
    face = index_ref.shape[1]
    group = coef_recv.shape[1]
    step = 512
    blocks = order // step
    ahead = AHEAD * (face // TICKS)

    loads_copy = pltpu.make_async_copy(loads_hbm, loads_ref, local_sems.at[0])
    tile_copy = pltpu.make_async_copy(tile_hbm, tile_ref, local_sems.at[1])
    op_copy = pltpu.make_async_copy(op_hbm, op_ref, local_sems.at[2])
    loads_copy.start()
    tile_copy.start()
    op_copy.start()

    sides = (
        (row > 0, (row - 1, col)),
        (row < rows - 1, (row + 1, col)),
        (col > 0, (row, col - 1)),
        (col < cols - 1, (row, col + 1)),
    )
    coef_col = (row * cols + col) // group
    coef_slot = lax.rem(col, group)
    source_row = (col * group) // cols
    source_col = lax.rem(col * group, cols)
    at_home = coef_col == col

    barrier = pltpu.get_barrier_semaphore()
    for k in range(1, cols):
        pl.semaphore_signal(
            barrier, inc=1, device_id=(row, lax.rem(col + k, cols)), device_id_type=MESH
        )
    for k in range(1, rows):
        pl.semaphore_signal(
            barrier, inc=1, device_id=(lax.rem(row + k, rows), col), device_id_type=MESH
        )
    for k in range(group):
        is_me = (source_row == row) & (source_col + k == col)

        @pl.when(jnp.logical_not(is_me))
        def _():
            pl.semaphore_signal(
                barrier, inc=1, device_id=(source_row, source_col + k), device_id_type=MESH
            )

    for f in range(4):

        @pl.when(jnp.logical_not(sides[f][0]))
        def _():
            mode_recv[f] = jnp.zeros(mode_recv.shape[1:], F32)
            face_recv[f] = jnp.zeros(face_recv.shape[1:], F32)
            for it in range(ITERS):
                product_recv[it, f] = jnp.zeros(product_recv.shape[2:], F32)
                amount_recv[it, f] = jnp.zeros(amount_recv.shape[2:], F32)

    def side_copy(f, source, target, sems):
        return pltpu.make_async_remote_copy(
            src_ref=source,
            dst_ref=target.at[f ^ 1],
            send_sem=sems.at[0, f],
            recv_sem=sems.at[1, f ^ 1],
            device_id=sides[f][1],
            device_id_type=MESH,
        )

    def start_side(f, source, target, sems):
        @pl.when(sides[f][0])
        def _():
            side_copy(f, source, target, sems).start()

    def wait_side(f, target, sems):
        @pl.when(sides[f][0])
        def _():
            pltpu.make_async_remote_copy(
                src_ref=target.at[f],
                dst_ref=target.at[f],
                send_sem=sems.at[0, f],
                recv_sem=sems.at[1, f],
                device_id=sides[f][1],
                device_id_type=MESH,
            ).wait_recv()

    def sent_side(f, source, target, sems):
        @pl.when(sides[f][0])
        def _():
            side_copy(f, source, target, sems).wait_send()

    def fill_pick(faces):
        for f in faces:
            down = jnp.broadcast_to(index_ref[f : f + 1, :], (LANES, face)).T

            @pl.loop(0, order // LANES)
            def _(i):
                there = lax.broadcasted_iota(jnp.int32, (face, LANES), 1) + i * LANES
                at = pl.ds(pl.multiple_of(i * LANES, LANES), LANES)
                pick[f * face : (f + 1) * face, at] = jnp.where(down == there, 1.0, 0.0).astype(
                    BF16
                )

    def make_modes():
        high, low = halves(modes_ref[...])
        modes_high[0:mode_count] = high
        modes_low[0:mode_count] = low
        both = jnp.concatenate([high, low], axis=0)
        for f in range(4):
            moved = lax.dot_general(
                both,
                pick[f * face : (f + 1) * face, :],
                (((1,), (1,)), ((), ())),
                preferred_element_type=F32,
            )
            mode_send[f] = moved[0:mode_count] + moved[mode_count:]

    def greet():
        here = (source_row == row) & (source_col <= col) & (col < source_col + group)
        greeted = cols - 1 + rows - 1 + group - here.astype(jnp.int32)
        pl.semaphore_wait(barrier, greeted)

    def modes_op():
        both = jnp.concatenate([modes_high[...], modes_low[...]], axis=0)
        count = modes_high.shape[0]

        @pl.loop(0, order // step)
        def _(i):
            at = pl.ds(pl.multiple_of(i * step, step), step)
            moved = mul(both, op_ref[:, at])
            high, low = halves(moved[0:count] + moved[count:])
            mode_op_high[:, at] = high
            mode_op_low[:, at] = low

    def pick_op():
        both = jnp.concatenate([pick[0:ahead, :], pick[face : face + ahead, :]], axis=0)

        @pl.loop(0, order // step)
        def _(i):
            at = pl.ds(pl.multiple_of(i * step, step), step)
            face_op[:, at] = mul(both, op_ref[:, at]).astype(BF16)

    def fill_place():
        @pl.loop(0, order // 256)
        def _(i):
            at = pl.ds(pl.multiple_of(i * 256, 256), 256)
            for f in range(4):
                here = lax.broadcasted_iota(jnp.int32, (256, face), 0) + i * 256
                hit = here == index_ref[f : f + 1, :]
                place[at, f * face : (f + 1) * face] = jnp.where(hit, 1.0, 0.0).astype(BF16)

    seam = cols // 2
    crossing = {2: col == seam, 3: col == seam - 1}
    over = {2: 1, 3: cols - 2}
    around = {2: (1,), 3: (0, 1)}
    short = face // 2

    def lateral(f, part, incoming):
        at = pl.ds(part * short, short)
        return pltpu.make_async_remote_copy(
            src_ref=face_recv.at[f, at] if incoming else face_send.at[f, at],
            dst_ref=face_recv.at[f if incoming else f ^ 1, at],
            send_sem=face_sems.at[0, f, part],
            recv_sem=face_sems.at[1, f if incoming else f ^ 1, part],
            device_id=sides[f][1],
            device_id_type=MESH,
        )

    def detour(f, part):
        at = pl.ds(part * short, short)
        return pltpu.make_async_remote_copy(
            src_ref=face_send.at[f, at],
            dst_ref=passing.at[at],
            send_sem=face_sems.at[0, f, part],
            recv_sem=pass_sems.at[0, part],
            device_id=(row, over[f]),
            device_id_type=MESH,
        )

    def onward(f, part):
        at = pl.ds(part * short, short)
        return pltpu.make_async_remote_copy(
            src_ref=passing.at[at],
            dst_ref=face_recv.at[f ^ 1, at],
            send_sem=pass_sems.at[1, part],
            recv_sem=face_sems.at[1, f ^ 1, part],
            device_id=(row, seam - 1 if f == 2 else seam),
            device_id_type=MESH,
        )

    def start_lateral(f):
        for part in range(2):
            if part in around[f]:

                @pl.when(sides[f][0] & jnp.logical_not(crossing[f]))
                def _():
                    lateral(f, part, False).start()

                @pl.when(crossing[f])
                def _():
                    detour(f, part).start()

            else:

                @pl.when(sides[f][0])
                def _():
                    lateral(f, part, False).start()

    def pass_lateral():
        for f in (2, 3):

            @pl.when(col == over[f])
            def _():
                for part in around[f]:
                    detour(f, part).wait_recv()
                    onward(f, part).start()

    def wait_lateral(f):
        for part in range(2):

            @pl.when(sides[f][0])
            def _():
                lateral(f, part, True).wait_recv()

    def sent_lateral(f):
        for part in range(2):

            @pl.when(sides[f][0])
            def _():
                lateral(f, part, False).wait_send()

        @pl.when(col == over[f])
        def _():
            for part in around[f]:
                onward(f, part).wait_send()

    def strip(it, f, j, incoming):
        tall = face // TICKS
        at = pl.ds(j * tall, tall)
        if incoming:
            source = face_recv.at[f, at]
            target = source
            arrived = f
        else:
            source = face_send.at[f, at]
            target = face_recv.at[f ^ 1, at]
            arrived = f ^ 1
        return pltpu.make_async_remote_copy(
            src_ref=source,
            dst_ref=target,
            send_sem=strip_sems.at[0, f, j],
            recv_sem=strip_sems.at[1, arrived, j],
            device_id=sides[f][1],
            device_id_type=MESH,
        )

    def tick(it, point):
        for j in SCHEDULE[it].get(point, ()):
            for f in range(2):

                @pl.when(sides[f][0])
                def _():
                    strip(it, f, j, False).start()

    def wait_strips(it, *ticks):
        for j in ticks:
            for f in range(2):

                @pl.when(sides[f][0])
                def _():
                    strip(it, f, j, True).wait_recv()

    def sent_strips(it):
        for j in range(TICKS):
            for f in range(2):

                @pl.when(sides[f][0])
                def _():
                    strip(it, f, j, False).wait_send()

    def each_block(body):
        @pl.loop(0, blocks)
        def _(i):
            body(pl.ds(pl.multiple_of(i * step, step), step))

    def negate(at):
        value = -loads_ref[at, :]
        field[at, :] = value
        high, low = halves(value)
        pieces[at, 0:cases] = high
        pieces[at, cases:] = low

    def faces_of_field(it, faces):
        for f in faces:
            moved = mul(pick[f * face : (f + 1) * face, :], pieces[...])
            face_send[f] = moved[:, 0:cases] + moved[:, cases:]

    def flag(f):
        return adj_ref[0, f].astype(F32)

    def fill_modes():
        for f in range(4):
            high, low = halves(mode_recv[f])
            moved = mul(
                jnp.concatenate([high, low], axis=0), pick[f * face : (f + 1) * face, :]
            )
            high, low = halves(moved[0:mode_count] + moved[mode_count:])
            at = slice((f + 1) * mode_count, (f + 2) * mode_count)
            modes_high[at] = high
            modes_low[at] = low
        modes_high_t[...] = modes_high[...].astype(F32).T.astype(BF16)
        modes_low_t[...] = modes_low[...].astype(F32).T.astype(BF16)

    def fill_rows():
        flags = jnp.concatenate(
            [jnp.full((face, LANES), flag(f), F32) for f in range(4)], axis=0
        ).astype(BF16)
        for i in range(blocks):
            glued = mul(place[i * step : (i + 1) * step, :], flags)
            touching = (
                jnp.broadcast_to(contact_ref[:, i * step : (i + 1) * step], (LANES, step))
                .astype(F32)
                .T
            )
            free = 1.0 - glued
            row_weight[i * step : (i + 1) * step, :] = 0.5 + 0.5 * free
            floor = jnp.where(touching * free > 0.5, 0.0, LOWEST)
            row_floor[i * step : (i + 1) * step, :] = floor

    def clamped(at, value):
        return jnp.maximum(value, wide(row_floor[at, :]))

    def all_sum(it, totals):
        parts = cases // LANES
        tile = jnp.concatenate(
            [totals[t : t + 1, p * LANES : (p + 1) * LANES] for t in range(2) for p in range(parts)]
            + [jnp.zeros((8 - 2 * parts, LANES), F32)],
            axis=0,
        )
        first_send[it] = tile

        def first(k):
            return pltpu.make_async_remote_copy(
                src_ref=first_send.at[it],
                dst_ref=first_recv.at[it, k],
                send_sem=first_sems.at[0, k],
                recv_sem=first_sems.at[1, k],
                device_id=(row, lax.rem(col + k, cols)),
                device_id_type=MESH,
            )

        for k in range(1, cols):
            first(k).start()
        for k in range(1, cols):
            first(k).wait_recv()
        tile = tile + first_recv[it, 1:cols].sum(axis=0)
        second_send[it] = tile

        def second(k):
            return pltpu.make_async_remote_copy(
                src_ref=second_send.at[it],
                dst_ref=second_recv.at[it, k],
                send_sem=second_sems.at[0, k],
                recv_sem=second_sems.at[1, k],
                device_id=(lax.rem(row + k, rows), col),
                device_id_type=MESH,
            )

        for k in range(1, rows):
            second(k).start()
        for k in range(1, rows):
            second(k).wait_recv()
        tile = tile + second_recv[it, 1:rows].sum(axis=0)
        for k in range(1, cols):
            first(k).wait_send()
        for k in range(1, rows):
            second(k).wait_send()
        top = jnp.concatenate([tile[p : p + 1] for p in range(parts)], axis=1)
        low = jnp.concatenate([tile[parts + p : parts + p + 1] for p in range(parts)], axis=1)
        return top / low

    for it in range(ITERS):
        if it == 0:
            fill_pick((0, 1, 2, 3))
            make_modes()
            greet()
            for f in range(4):
                start_side(f, mode_send.at[f], mode_recv, mode_sems)
            loads_copy.wait()
            each_block(negate)
            faces_of_field(it, (0, 1))
            tick(it, "faces")
            faces_of_field(it, (2, 3))
            for f in range(4):
                wait_side(f, mode_recv, mode_sems)
            for f in range(4):
                mode_recv[f] = mode_recv[f] * flag(f)
            for f in range(4):
                product_send[it, f] = mul_split(halves(mode_recv[f]), halves(face_send[f]))
            for f in range(4):
                start_side(f, product_send.at[it, f], product_recv.at[it], product_sems)
            tick(it, "products")
            for f in (2, 3):
                start_lateral(f)
            fill_place()
            own = mul_split(
                (modes_high[0:mode_count], modes_low[0:mode_count]),
                (pieces[:, 0:cases], pieces[:, cases:]),
            )
            first_own[...] = own
        else:
            own = next_own
        for f in range(4):
            wait_side(f, product_recv.at[it], product_sems)
            own = own + product_recv[it, f]
        coef_send[it] = own

        def coef(k):
            return pltpu.make_async_remote_copy(
                src_ref=coef_send.at[it],
                dst_ref=coef_recv.at[it, coef_slot],
                send_sem=coef_sems.at[0, k],
                recv_sem=coef_sems.at[1, coef_slot],
                device_id=(lax.rem(row + k, rows), coef_col),
                device_id_type=MESH,
            )

        for k in range(rows):
            if k == 0:

                @pl.when(at_home)
                def _():
                    coef_recv[it, coef_slot] = own

                @pl.when(jnp.logical_not(at_home))
                def _():
                    coef(0).start()

            else:
                coef(k).start()
        tick(it, "coefs")
        if it == 1:
            faces_of_field(it, (2, 3))
            for f in (2, 3):
                start_lateral(f)
        if it == 0:
            fill_modes()
            fill_rows()
            op_copy.wait()
            pick_op()
            modes_op()
            tile_copy.wait()
        tick(it, "fill")
        for k in range(group):
            is_me = (source_row == row) & (source_col + k == col)

            @pl.when(jnp.logical_not(is_me))
            def _():
                pltpu.make_async_remote_copy(
                    src_ref=coef_send.at[it],
                    dst_ref=coef_recv.at[it, k],
                    send_sem=coef_sems.at[0, 0],
                    recv_sem=coef_sems.at[1, k],
                    device_id=(source_row, source_col + k),
                    device_id_type=MESH,
                ).wait_recv()

        block = coef_recv[it].reshape(group * mode_count, cases)
        partial = mul_split(halves(tile_ref[...]), halves(block)).reshape(
            cols // 2, 2, mode_count, cases
        )
        part_send[it, 0] = partial[:, 0]
        part_send[it, 1] = partial[:, 1]
        core = lax.rem(col, 2)
        pair = pltpu.make_async_remote_copy(
            src_ref=part_send.at[it, 1 - core],
            dst_ref=pair_recv.at[it],
            send_sem=pair_sems.at[0],
            recv_sem=pair_sems.at[1],
            device_id=(row, col + 1 - 2 * core),
            device_id_type=MESH,
        )
        pair.start()
        pair.wait_recv()
        pair_send[it] = part_send[it, core] + pair_recv[it]

        def part(k):
            target = lax.rem(col + 2 * k, cols)
            return pltpu.make_async_remote_copy(
                src_ref=pair_send.at[it, target // 2],
                dst_ref=part_recv.at[it, k],
                send_sem=part_sems.at[0, k],
                recv_sem=part_sems.at[1, k],
                device_id=(row, target),
                device_id_type=MESH,
            )

        for k in range(1, cols // 2):
            part(k).start()
        def spread(f, at):
            high, low = halves(face_recv[f, at] * flag(f))
            return jnp.concatenate([high, low], axis=1)

        def add_sides():
            for f in (2, 3):
                pieces[f * face : (f + 1) * face, :] = spread(f, slice(0, face))

            def add(at):
                moved = mul(place[at, 2 * face : 4 * face], pieces[2 * face : 4 * face, :])
                field[at, :] = field[at, :] + (moved[:, 0:cases] + moved[:, cases:])

            each_block(add)

        def strips(j):
            tall = 2 * (face // TICKS)
            span = slice(j // 2 * tall, (j // 2 + 1) * tall)
            lower = slice(face + j // 2 * tall, face + (j // 2 + 1) * tall)
            wait_strips(it, j, j + 1)
            return span, lower, jnp.concatenate([spread(0, span), spread(1, span)], axis=0)

        def add_strips(j):
            span, lower, both = strips(j)

            def add(at):
                there = jnp.concatenate([place[at, span], place[at, lower]], axis=1)
                moved = mul(there, both)
                field[at, :] = field[at, :] + (moved[:, 0:cases] + moved[:, cases:])

            each_block(add)

        tick(it, "parts")
        pass_lateral()
        for j in range(0, EARLY[it], 2):
            add_strips(j)
        for k in range(1, cols // 2):
            part(k).wait_recv()
        amount = pair_send[it, col // 2] + part_recv[it, 1 : cols // 2].sum(axis=0)
        amount_send[it] = amount
        for f in range(4):
            start_side(f, amount_send.at[it], amount_recv.at[it], amount_sems)
        tick(it, "amounts")
        for f in (2, 3):
            wait_lateral(f)
        add_sides()
        for j in range(EARLY[it], TICKS - 2, 2):
            add_strips(j)
        for f in range(4):
            wait_side(f, amount_recv.at[it], amount_sems)
        amounts = halves(
            jnp.concatenate([amount] + [amount_recv[it, f] for f in range(4)], axis=0)
        )

        def correct(at):
            field[at, :] = field[at, :] - mul_split(
                (modes_high_t[at, :], modes_low_t[at, :]), amounts
            )

        each_block(correct)
        last, lower, both = strips(TICKS - 2)

        def turn(i, total):
            at = pl.ds(pl.multiple_of(i * step, step), step)
            there = jnp.concatenate([place[at, last], place[at, lower]], axis=1)
            moved = mul(there, both)
            value = field[at, :] + (moved[:, 0:cases] + moved[:, cases:])
            direction[at, :] = value
            direction_half[at, :] = value.astype(BF16)
            return total + by_eight(wide(row_weight[at, :]) * value * value)

        top = lax.fori_loop(0, blocks, turn, jnp.zeros((8, cases), F32))
        def operate(i, total):
            at = pl.ds(pl.multiple_of(i * step, step), step)
            return total + by_eight(direction[at, :] * mul(op_ref[at, :], direction_half[...]))

        low = lax.fori_loop(0, blocks, operate, jnp.zeros((8, cases), F32))
        totals = jnp.concatenate(
            [top.sum(axis=0, keepdims=True), low.sum(axis=0, keepdims=True)], axis=0
        )
        for f in range(4):
            if it == 0:
                sent_side(f, mode_send.at[f], mode_recv, mode_sems)
            sent_side(f, product_send.at[it, f], product_recv.at[it], product_sems)
            if f >= 2:
                sent_lateral(f)
            sent_side(f, amount_send.at[it], amount_recv.at[it], amount_sems)
        for k in range(rows):
            if k == 0:

                @pl.when(jnp.logical_not(at_home))
                def _():
                    coef(0).wait_send()

            else:
                coef(k).wait_send()
        for k in range(1, cols // 2):
            part(k).wait_send()
        pair.wait_send()
        sent_strips(it)
        length = all_sum(it, totals)

        if it == 0:

            def first_update(at):
                value = clamped(at, 0.0 - length * direction[at, :])
                first_value[at, :] = value
                direction_half[at, :] = value.astype(BF16)

            each_block(first_update)
            products = mul(mode_op_high[...], direction_half[...]) + mul(
                mode_op_low[...], direction_half[...]
            )
            next_own = products[0:mode_count] + first_own[...]
            for f in range(4):
                at = slice((f + 1) * mode_count, (f + 2) * mode_count)
                product_send[it + 1, f] = products[at] + product_send[it, f]
            for f in range(4):
                start_side(f, product_send.at[it + 1, f], product_recv.at[it + 1], product_sems)
            moved = mul(face_op[...], direction_half[...])
            for f in (0, 1):
                face_send[f, 0:ahead] = face_send[f, 0:ahead] + moved[f * ahead : (f + 1) * ahead]
            tick(it + 1, "faces")

            def local_term(at):
                value = mul(op_ref[at, :], direction_half[...]) - loads_ref[at, :]
                field[at, :] = value
                high, low = halves(value)
                pieces[at, 0:cases] = high
                pieces[at, cases:] = low

            each_block(local_term)
            for f in (0, 1):
                moved = mul(pick[f * face + ahead : (f + 1) * face, :], pieces[...])
                face_send[f, ahead:] = moved[:, 0:cases] + moved[:, cases:]
            tick(it + 1, "sides")
        else:

            def out_copy(i):
                at = slice(i * step, (i + 1) * step)
                return pltpu.make_async_copy(field.at[at], out_hbm.at[at], local_sems.at[3 + i])

            for i in range(blocks):
                at = slice(i * step, (i + 1) * step)
                field[at, :] = clamped(at, first_value[at, :] - length * direction[at, :])
                out_copy(i).start()

    for i in range(blocks):
        out_copy(i).wait()


def per_device(rows, cols, local_ops, loads, modes, coarse_inverse, face_rows, adjacency, contact):
    order, cases = loads.shape[2:]
    mode_count = modes.shape[2]
    face = face_rows.shape[3]
    group = coarse_inverse.shape[1] // mode_count
    stack = 5 * mode_count
    vmem = pl.BlockSpec(memory_space=pltpu.VMEM)
    dma = pltpu.SemaphoreType.DMA
    scratch = [
        pltpu.VMEM((order, cases), F32),
        pltpu.VMEM(coarse_inverse.shape, F32),
        pltpu.VMEM((order, order), BF16),
        pltpu.VMEM((order, order), BF16),
        pltpu.VMEM((order, order), BF16),
        pltpu.VMEM((2 * AHEAD * (face // TICKS), order), BF16),
        pltpu.VMEM((stack, order), BF16),
        pltpu.VMEM((stack, order), BF16),
        pltpu.VMEM((mode_count, cases), F32),
        pltpu.VMEM((order, 2 * cases), BF16),
        pltpu.VMEM((stack, order), BF16),
        pltpu.VMEM((stack, order), BF16),
        pltpu.VMEM((order, stack), BF16),
        pltpu.VMEM((order, stack), BF16),
        pltpu.VMEM((order, LANES), F32),
        pltpu.VMEM((order, LANES), F32),
        pltpu.VMEM((order, cases), F32),
        pltpu.VMEM((order, cases), F32),
        pltpu.VMEM((order, cases), F32),
        pltpu.VMEM((order, cases), BF16),
        pltpu.VMEM((4, mode_count, face), F32),
        pltpu.VMEM((4, mode_count, face), F32),
        pltpu.VMEM((4, face, cases), F32),
        pltpu.VMEM((4, face, cases), F32),
        pltpu.VMEM((face, cases), F32),
        pltpu.VMEM((ITERS, 4, mode_count, cases), F32),
        pltpu.VMEM((ITERS, 4, mode_count, cases), F32),
        pltpu.VMEM((ITERS, mode_count, cases), F32),
        pltpu.VMEM((ITERS, group, mode_count, cases), F32),
        pltpu.VMEM((ITERS, 2, cols // 2, mode_count, cases), F32),
        pltpu.VMEM((ITERS, cols // 2, mode_count, cases), F32),
        pltpu.VMEM((ITERS, cols // 2, mode_count, cases), F32),
        pltpu.VMEM((ITERS, cols // 2, mode_count, cases), F32),
        pltpu.VMEM((ITERS, mode_count, cases), F32),
        pltpu.VMEM((ITERS, 4, mode_count, cases), F32),
        pltpu.VMEM((ITERS, 8, LANES), F32),
        pltpu.VMEM((ITERS, cols, 8, LANES), F32),
        pltpu.VMEM((ITERS, 8, LANES), F32),
        pltpu.VMEM((ITERS, rows, 8, LANES), F32),
        dma((3 + 4,)),
        dma((2, 4)),
        dma((2, 4, 2)),
        dma((2, 2)),
        dma((2, 2, TICKS)),
        dma((2, 4)),
        dma((2, max(rows, group))),
        dma((2,)),
        dma((2, cols // 2)),
        dma((2, 4)),
        dma((2, cols)),
        dma((2, rows)),
    ]
    anywhere = pl.BlockSpec(memory_space=pl.ANY)
    result = pl.pallas_call(
        functools.partial(kernel, rows, cols),
        out_shape=jax.ShapeDtypeStruct((order, cases), F32),
        in_specs=[pl.BlockSpec(memory_space=pltpu.SMEM)]
        + [vmem] * 3
        + [anywhere] * 3,
        out_specs=anywhere,
        scratch_shapes=scratch,
        compiler_params=pltpu.CompilerParams(
            collective_id=0, has_side_effects=True, vmem_limit_bytes=VMEM_BYTES
        ),
        name="dual_steps",
    )(
        adjacency[0],
        modes[0, 0],
        face_rows[0, 0],
        contact[0],
        loads[0, 0],
        coarse_inverse,
        local_ops[0, 0],
    )
    return result[None, None]


def solution(mesh):
    rows, cols = mesh.shape["row"], mesh.shape["col"]
    return jax.shard_map(
        functools.partial(per_device, rows, cols),
        mesh=mesh,
        in_specs=(
            P("row", "col", None, None),
            P("row", "col", None, None),
            P("row", "col", None, None),
            P("row", "col"),
            P("row", "col", None, None),
            P("row", "col", None),
            P("row", "col", None),
        ),
        out_specs=P("row", "col", None, None),
        check_vma=False,
    )
```
